512 devices in a mesh: dp: 16 (over y, z_lo), expert: 32 (over x, z_hi, core).
Axes of the slice: x: 4, y: 4, z: 16 (z_hi: 4, z_lo: 4; z = z_hi * 4 + z_lo), core: 2. Of those that a mesh axis runs over, the one named last changes fastest.
Arguments:
- tokens: bfloat16 [65536, 2048], P(('dp', 'expert')), may hold values from -6 to 6
- out_grad: bfloat16 [65536, 2048], P(('dp', 'expert')), may hold values from -24 to 24
- routing: int32 [65536, 2], P(('dp', 'expert')), may hold values from 0 to 31, all different within a row; in each aligned block of 128 rows (0 to 127, 128 to 255, ...) at most 9 rows name the same one
- gate_probs: float32 [65536, 2], P(('dp', 'expert')), may hold values from 0.1 to 1
- gate_up_weight: bfloat16 [32, 2048, 1536], P('expert', 'dp'), may hold values from -0.125 to 0.125
- down_weight: bfloat16 [32, 2048, 768], P('expert', 'dp'), may hold values from -0.21875 to 0.21875
Outputs:
- mixed: bfloat16 [65536, 2048], P(('dp', 'expert'))
- token_grad: bfloat16 [65536, 2048], P(('dp', 'expert'))
- down_grad: bfloat16 [32, 2048, 768], P('expert', 'dp')
The draws below stay inside these ranges and needn't reach their ends.
Inputs may be any that keep to these rules, and one draw needn't show every extreme that they name: `routing`: the 2 ids of a row differ. Among the 128 rows of one device (aligned blocks) no id appears more than 9 times, and some id appears exactly 9 times.
All inputs are finite; a program needn't handle non-finite values.
Results may differ from the reference program's by a relative error of at most 0.018.
Values may be sent and summed in bfloat16 or wider, within the bound.
A program may use at most 64 MiB of HBM per device.

```python
import math
import jax
import jax.numpy as jnp
import numpy as np
from jax import lax

D = 2048
H = 768
TOP = 2
TOK_DEV = 128
EXPERTS = 32
CAP = 9
TOKENS = 65536
N_DP = 16
N_EXPERT = 32


def with_spikes(drawn, stream_key, source, target, parts, factor):
    owner, partner = [(jnp.arange(drawn.shape[position]) // (drawn.shape[position] // parts)).reshape([-1 if axis == position else 1 for axis in range(drawn.ndim)]) for position in (source, target)]
    chosen = jax.random.permutation(stream_key, parts)[partner]
    strong = (owner == chosen) | (owner == (partner + parts // 2) % parts)
    return jnp.where(strong, factor * drawn, drawn)


def levels(own_key, extent, split, least, top_value):
    def one(position, blocks):
        steps = jax.random.uniform(jax.random.fold_in(jax.random.fold_in(own_key, 6), position), (blocks,), jnp.float32, least / len(split), top_value / len(split))
        return jnp.repeat(jnp.exp(steps), extent[position] // blocks).reshape((-1,) + (1,) * (len(extent) - position - 1))

    loudness = one(*split[0])
    for cut in split[1:]:
        loudness = loudness * one(*cut)
    return loudness


def assign_block(own_key, own, number, rows, count, top, reach, lean):
    sequence = jax.random.permutation(own_key, count)
    packed, common = load_shares(count, rows * top, reach, lean, True), load_shares(count, rows * top, reach, lean, False)
    places = jnp.arange(count)

    def named(tallies, rotation):
        used = int((tallies > 0).sum())
        fixed = max(1, used // 4)
        moved = fixed + (places - fixed + rotation * (used - fixed)) % max(1, count - fixed)
        return jnp.zeros((count,), jnp.int32).at[sequence[jnp.where(places < fixed, places, moved)]].set(jnp.asarray(tallies, jnp.int32))

    tallies = jnp.where(number % 4 == 0, named(packed, number // 4), named(common, number - number // 4 - 1))
    mixed = jax.random.permutation(jax.random.fold_in(own, 3), count)
    donor, receiver = mixed[0:count // 2 * 2:2], mixed[1:count // 2 * 2:2]
    room = jnp.minimum(tallies[donor] - 1, reach - tallies[receiver]) // 2
    room = jnp.where((donor == sequence[0]) | (receiver == sequence[0]) | (tallies[receiver] == 0), 0, jnp.maximum(room, 0))
    moved = jax.random.randint(jax.random.fold_in(own, 4), (count // 2,), 0, 1 << 20) % (room + 1)
    tallies = tallies.at[donor].add(-moved).at[receiver].add(moved)
    members = jnp.searchsorted(jnp.cumsum(tallies), jnp.arange(rows * top), side="right").astype(jnp.int32)
    table = members.reshape(top, rows).T
    table = table[jax.random.permutation(jax.random.fold_in(own, 1), rows)]
    rotation = jax.random.randint(jax.random.fold_in(own, 2), (rows, 1), 0, top)
    return jnp.take_along_axis(table, (jnp.arange(top)[None, :] + rotation) % top, axis=1)


def load_shares(count, total, limit, slope, full):
    loads = [(1 << 20) // math.isqrt(rank ** slope) + 1 for rank in range(1, count + 1)]
    largest = limit if full else min(limit, max(-(-total // count), total * loads[0] // sum(loads)))
    least = 1 if total - largest >= count - 1 else 0
    holding, spare = [largest] + [least] * (count - 1), total - largest - least * (count - 1)
    while spare > 0:
        candidates = [i for i in range(1, count) if holding[i] < largest] or [i for i in range(1, count) if holding[i] < limit]
        mass, remaining = sum([loads[i] for i in candidates]), spare
        for i in candidates:
            extra = min(limit - holding[i], max(1, remaining * loads[i] // mass), spare)
            holding[i] = holding[i] + extra
            spare = spare - extra
    return np.array(holding)


def bell_draw(rng, dims, width, limit, split=(), kind=jnp.bfloat16):
    factor_of = levels(rng, dims, split, -0.22, 0.18) if split else 1.0
    array = jax.random.normal(rng, dims, jnp.float32) * width * factor_of
    return jnp.minimum(jnp.maximum(array, -limit), limit).astype(kind)


def bell_draw_with(own_key, extent, width, limit, shards, heavy, kind=jnp.bfloat16):
    result = width * jax.random.normal(own_key, extent, jnp.float32)
    if shards:
        result = result * levels(own_key, extent, shards, -0.22, 0.18)
    return jnp.clip(with_spikes(result, jax.random.fold_in(own_key, 3), *heavy), -limit, limit).astype(kind)


def setup_inputs(seed: int = 0) -> dict:
    splits = jax.random.split(jax.random.key(seed), 7)
    tokens = bell_draw(splits[0], (TOKENS, D), 1.0, 6.0, ((0, 512),))
    out_grad = bell_draw_with(splits[1], (TOKENS, D), 1.0, 24.0, ((0, 512),), (0, 1, 512, 6.0))
    routing_keys = jax.random.split(jax.random.fold_in(splits[2], 1), TOKENS // TOK_DEV)
    routing_turns = jax.random.permutation(jax.random.fold_in(splits[2], 3), TOKENS // TOK_DEV)
    routing = jax.vmap(lambda own, number: assign_block(jax.random.fold_in(splits[2], 2), own, number, TOK_DEV, EXPERTS, TOP, CAP, 1))(routing_keys, routing_turns).reshape((TOKENS, TOP))
    gate_probs = jnp.clip(0.1 + 0.9 * jax.random.uniform(splits[3], (TOKENS, TOP), jnp.float32) ** levels(splits[3], (TOKENS, TOP), ((0, 512),), -0.2, 0.2), 0.1, 1.0)
    gate_up_weight = bell_draw(splits[4], (EXPERTS, D, 2 * H), D ** -0.5, 0.125, ((0, 32), (1, 16)))
    down_weight = bell_draw(splits[5], (EXPERTS, D, H), H ** -0.5, 0.21875, ((0, 32), (1, 16)))
    return dict(tokens=tokens, out_grad=out_grad, routing=routing, gate_probs=gate_probs, gate_up_weight=gate_up_weight, down_weight=down_weight)


loss_scale = 0.03125


def reference(tokens, out_grad, routing, gate_probs, gate_up_weight, down_weight):
    groups = N_DP * N_EXPERT
    pair_count = TOK_DEV * TOP
    slot_count = EXPERTS * CAP
    flat_ids = routing.reshape(groups, pair_count)
    onehot = (flat_ids[:, :, None] == jnp.arange(EXPERTS, dtype=jnp.int32)[None, None, :]).astype(jnp.int32)
    slot_rank = jnp.sum((jnp.cumsum(onehot, 1) - onehot) * onehot, 2).astype(jnp.int32)
    slot_of_pair = (flat_ids * CAP + slot_rank).astype(jnp.int32)
    group_index = jnp.arange(groups, dtype=jnp.int32)[:, None]
    pair_index = jnp.broadcast_to(jnp.arange(pair_count, dtype=jnp.int32)[None, :], (groups, pair_count))
    source = jnp.full((groups, slot_count), pair_count, jnp.int32).at[group_index, slot_of_pair].set(pair_index)
    filled = source < pair_count
    source_clip = jnp.minimum(source, pair_count - 1).astype(jnp.int32)
    token_index = (group_index * TOK_DEV + source_clip // TOP).astype(jnp.int32)
    probs_flat = gate_probs.reshape(groups, pair_count)
    weight_slot = jnp.where(filled, jnp.take_along_axis(probs_flat, source_clip, axis=1), jnp.float32(0.0))

    def per_expert(table):
        return jnp.transpose(table.reshape(groups, EXPERTS, CAP), (1, 0, 2)).reshape(EXPERTS, groups * CAP)

    token_table = per_expert(token_index)
    filled_table = per_expert(filled)
    weight_table = per_expert(weight_slot)

    def expert_step(carry, inputs):
        mixed_acc, grad_acc = carry
        token_ids, slot_filled, slot_weight, gate_up_e, down_e = inputs
        gate_up_f = gate_up_e.astype(jnp.float32)
        down_f = down_e.astype(jnp.float32)
        expert_rows = tokens[token_ids].astype(jnp.float32)
        projected = jnp.dot(expert_rows, gate_up_f)
        gate_part = projected[:, :H]
        up_part = projected[:, H:]
        sigmoid_gate = jax.nn.sigmoid(gate_part)
        silu_gate = gate_part * sigmoid_gate
        hidden = (silu_gate * up_part).astype(jnp.bfloat16)
        expert_out = jnp.dot(hidden.astype(jnp.float32), down_f.T).astype(jnp.bfloat16)
        row_grad = (slot_weight[:, None] * out_grad[token_ids].astype(jnp.float32)).astype(jnp.bfloat16)
        hidden_grad = jnp.dot(row_grad.astype(jnp.float32), down_f)
        pre_grad = jnp.concatenate([hidden_grad * up_part * sigmoid_gate * (1.0 + gate_part * (1.0 - sigmoid_gate)), hidden_grad * silu_gate], axis=1).astype(jnp.bfloat16)
        input_grad = jnp.dot(pre_grad.astype(jnp.float32), gate_up_f.T).astype(jnp.bfloat16)
        live = slot_filled[:, None]
        mixed_acc = mixed_acc.at[token_ids].add(jnp.where(live, slot_weight[:, None] * expert_out.astype(jnp.float32), jnp.float32(0.0)))
        grad_acc = grad_acc.at[token_ids].add(jnp.where(live, input_grad.astype(jnp.float32), jnp.float32(0.0)))
        grad_groups = row_grad.astype(jnp.float32).reshape(N_DP, N_EXPERT * CAP, D)
        hidden_groups = hidden.astype(jnp.float32).reshape(N_DP, N_EXPERT * CAP, H)
        part_grad = (jnp.einsum("qrd,qrh->qdh", grad_groups, hidden_groups) * loss_scale).astype(jnp.bfloat16)
        down_grad_e = jnp.sum(part_grad.astype(jnp.float32), axis=0).astype(jnp.bfloat16)
        return (mixed_acc, grad_acc), down_grad_e

    start = (jnp.zeros((TOKENS, D), jnp.float32), jnp.zeros((TOKENS, D), jnp.float32))
    (mixed_acc, grad_acc), down_grad = lax.scan(expert_step, start, (token_table, filled_table, weight_table, gate_up_weight, down_weight))
    return mixed_acc.astype(jnp.bfloat16), grad_acc.astype(jnp.bfloat16), down_grad
```

```python
import jax
import jax.numpy as jnp
from jax import lax
from jax.sharding import PartitionSpec as P

loss_scale = 0.03125


def swiglu_forward(expert_rows, gate_up_full):
    projected = jnp.dot(expert_rows, gate_up_full, preferred_element_type=jnp.float32)
    units = gate_up_full.shape[1] // 2
    gate_part = projected[:, :units]
    up_part = projected[:, units:]
    sigmoid_gate = jax.nn.sigmoid(gate_part)
    silu_gate = gate_part * sigmoid_gate
    hidden = (silu_gate * up_part).astype(jnp.bfloat16)
    return (hidden, gate_part, up_part, sigmoid_gate, silu_gate)


def weight_term(grad_rows, hidden):
    product = lax.dot_general(
        grad_rows, hidden, (((0,), (0,)), ((), ())), preferred_element_type=jnp.float32
    )
    parts = lax.axis_size("dp")
    blocks = (product * loss_scale).astype(jnp.bfloat16)
    blocks = blocks.reshape(parts, blocks.shape[0] // parts, blocks.shape[1])
    received = lax.all_to_all(blocks, "dp", split_axis=0, concat_axis=0, tiled=True)
    return jnp.sum(received.astype(jnp.float32), axis=0)


def gather_rows(local):
    parts = lax.axis_size("dp")
    copies = jnp.broadcast_to(local[None], (parts,) + local.shape)
    received = lax.all_to_all(copies, "dp", split_axis=0, concat_axis=0, tiled=True)
    return received.reshape(parts * local.shape[0], local.shape[1])


def shards(tokens, out_grad, routing, gate_probs, gate_up_weight, down_weight):
    peer_count = lax.axis_size("expert")
    local_count = gate_up_weight.shape[0]
    expert_count = peer_count * local_count
    tok_rows = tokens.shape[0]
    top_count = routing.shape[1]
    model_width = tokens.shape[1]
    capacity = max(2, 9 * tok_rows * top_count // (8 * expert_count))
    pair_count = tok_rows * top_count
    slot_count = expert_count * capacity
    flat_ids = routing.reshape(pair_count)
    onehot = (flat_ids[:, None] == jnp.arange(expert_count, dtype=jnp.int32)[None, :]).astype(
        jnp.int32
    )
    slot_rank = jnp.sum((jnp.cumsum(onehot, 0) - onehot) * onehot, 1)
    slot_of_pair = flat_ids * capacity + slot_rank
    pair_index = jnp.arange(pair_count, dtype=jnp.int32)
    matches = slot_of_pair[None, :] == jnp.arange(slot_count, dtype=jnp.int32)[:, None]
    filled = jnp.any(matches, axis=1)
    source = jnp.sum(jnp.where(matches, pair_index[None, :], 0), axis=1)
    token_of_slot = source // top_count
    probs_flat = gate_probs.reshape(pair_count)
    weight_slot = jnp.where(filled, probs_flat[source], jnp.float32(0.0))
    send_rows = jnp.where(filled[:, None], tokens[token_of_slot], jnp.zeros((), jnp.bfloat16))
    send_grad = (weight_slot[:, None] * out_grad[token_of_slot].astype(jnp.float32)).astype(
        jnp.bfloat16
    )
    block_shape = (peer_count, local_count * capacity, model_width)
    recv_rows, recv_grad = (
        lax.all_to_all(
            send_rows.reshape(block_shape), "expert", split_axis=0, concat_axis=0, tiled=True
        ),
        lax.all_to_all(
            send_grad.reshape(block_shape), "expert", split_axis=0, concat_axis=0, tiled=True
        ),
    )
    gate_width = gate_up_weight.shape[2]
    joined = jnp.concatenate([gate_up_weight[0], down_weight[0]], axis=1)
    full_joined = gather_rows(joined)
    full_gate_up = full_joined[None, :, :gate_width]
    full_down = full_joined[None, :, gate_width:]
    expert_slot = 0
    expert_rows = recv_rows.reshape(-1, model_width)
    state = swiglu_forward(expert_rows, full_gate_up[expert_slot])
    forward_state = [state]
    produced = lax.dot_general(
        state[0],
        full_down[expert_slot],
        (((1,), (1,)), ((), ())),
        preferred_element_type=jnp.float32,
    )
    output_blocks = produced.astype(jnp.bfloat16).reshape(peer_count, capacity, model_width)
    expert_slot = 0
    grad_rows = recv_grad.reshape(-1, model_width)
    hidden, gate_part, up_part, sigmoid_gate, silu_gate = forward_state[expert_slot]
    down_terms = [weight_term(grad_rows, hidden)]
    hidden_grad = jnp.dot(grad_rows, full_down[expert_slot], preferred_element_type=jnp.float32)
    pre_grad = jnp.concatenate(
        [
            hidden_grad * up_part * sigmoid_gate * (1.0 + gate_part * (1.0 - sigmoid_gate)),
            hidden_grad * silu_gate,
        ],
        axis=1,
    ).astype(jnp.bfloat16)
    input_grad = lax.dot_general(
        pre_grad,
        full_gate_up[expert_slot],
        (((1,), (1,)), ((), ())),
        preferred_element_type=jnp.float32,
    )
    grad_blocks = input_grad.astype(jnp.bfloat16).reshape(peer_count, capacity, model_width)
    returned_out, returned_grad = (
        lax.all_to_all(output_blocks, "expert", split_axis=0, concat_axis=0, tiled=True),
        lax.all_to_all(grad_blocks, "expert", split_axis=0, concat_axis=0, tiled=True),
    )
    out_pairs = returned_out.reshape(slot_count, model_width)[slot_of_pair]
    grad_pairs = returned_grad.reshape(slot_count, model_width)[slot_of_pair]
    weighted = probs_flat[:, None] * out_pairs.astype(jnp.float32)
    mixed = jnp.sum(weighted.reshape(tok_rows, top_count, model_width), axis=1).astype(jnp.bfloat16)
    token_grad = jnp.sum(
        grad_pairs.astype(jnp.float32).reshape(tok_rows, top_count, model_width), axis=1
    ).astype(jnp.bfloat16)
    down_grad = jnp.stack(down_terms, axis=0).astype(jnp.bfloat16)
    return (mixed, token_grad, down_grad)


def solution(mesh):
    in_specs = (
        P(("dp", "expert"), None),
        P(("dp", "expert"), None),
        P(("dp", "expert"), None),
        P(("dp", "expert"), None),
        P("expert", "dp", None),
        P("expert", "dp", None),
    )
    out_specs = (P(("dp", "expert"), None), P(("dp", "expert"), None), P("expert", "dp", None))
    return jax.shard_map(shards, mesh=mesh, in_specs=in_specs, out_specs=out_specs, check_vma=False)
```

```python
import functools

import jax
import jax.numpy as jnp
from jax import lax
from jax.experimental import pallas as pl
from jax.experimental.pallas import tpu as pltpu
from jax.sharding import PartitionSpec as P

MESH = pl.DeviceIdType.MESH

loss_scale = 0.03125


def exchange_kernel(n_dp, n_ex, bcast, ex_send, dp_send, ex_recv, dp_recv, send_sems, recv_sems, own_sems):
    q = lax.axis_index("dp")
    p = lax.axis_index("expert")
    barrier = pltpu.get_barrier_semaphore()

    def greet_ex(k, c):
        pl.semaphore_signal(barrier, 1, device_id=(q, lax.rem(p + k, n_ex)), device_id_type=MESH)
        return c

    def greet_dp(k, c):
        pl.semaphore_signal(barrier, 1, device_id=(lax.rem(q + k, n_dp), p), device_id_type=MESH)
        return c

    lax.fori_loop(1, n_ex, greet_ex, 0)
    lax.fori_loop(1, n_dp, greet_dp, 0)
    pl.semaphore_wait(barrier, n_ex + n_dp - 2)

    def ex_copy(j, slot):
        return pltpu.make_async_remote_copy(
            src_ref=ex_send.at[j], dst_ref=ex_recv.at[slot], send_sem=send_sems.at[j],
            recv_sem=recv_sems.at[slot], device_id=(q, j), device_id_type=MESH)

    def dp_copy(i, slot):
        src = dp_send if bcast else dp_send.at[i]
        return pltpu.make_async_remote_copy(
            src_ref=src, dst_ref=dp_recv.at[slot], send_sem=send_sems.at[n_ex + i],
            recv_sem=recv_sems.at[n_ex + slot], device_id=(i, p), device_id_type=MESH)

    def send_ex(k, c):
        ex_copy(lax.rem(p + k, n_ex), p).start()
        return c

    def send_dp(k, c):
        dp_copy(lax.rem(q + k, n_dp), q).start()
        return c

    lax.fori_loop(1, n_dp, send_dp, 0)
    lax.fori_loop(1, n_ex, send_ex, 0)
    own_ex = pltpu.make_async_copy(ex_send.at[p], ex_recv.at[p], own_sems.at[0])
    own_dp = pltpu.make_async_copy(dp_send if bcast else dp_send.at[q], dp_recv.at[q], own_sems.at[1])
    own_ex.start()
    own_dp.start()

    def wait_ex(k, c):
        j = lax.rem(p + k, n_ex)
        ex_copy(j, p).wait_send()
        ex_copy(j, j).wait_recv()
        return c

    def wait_dp(k, c):
        i = lax.rem(q + k, n_dp)
        dp_copy(i, q).wait_send()
        dp_copy(i, i).wait_recv()
        return c

    lax.fori_loop(1, n_ex, wait_ex, 0)
    lax.fori_loop(1, n_dp, wait_dp, 0)
    own_ex.wait()
    own_dp.wait()


def exchange(ex_send, dp_send, bcast, cid):
    n_dp = lax.axis_size("dp")
    n_ex = lax.axis_size("expert")
    dp_block = dp_send.shape if bcast else dp_send.shape[1:]
    return pl.pallas_call(
        functools.partial(exchange_kernel, n_dp, n_ex, bcast),
        out_shape=(
            jax.ShapeDtypeStruct(ex_send.shape, ex_send.dtype),
            jax.ShapeDtypeStruct((n_dp,) + tuple(dp_block), dp_send.dtype),
        ),
        in_specs=[pl.BlockSpec(memory_space=pl.ANY)] * 2,
        out_specs=(pl.BlockSpec(memory_space=pl.ANY), pl.BlockSpec(memory_space=pl.ANY)),
        scratch_shapes=[
            pltpu.SemaphoreType.DMA((n_ex + n_dp,)),
            pltpu.SemaphoreType.DMA((n_ex + n_dp,)),
            pltpu.SemaphoreType.DMA((2,)),
        ],
        compiler_params=pltpu.CompilerParams(collective_id=cid, has_side_effects=True),
    )(ex_send, dp_send)


def swiglu_forward(expert_rows, gate_up_full):
    projected = jnp.dot(expert_rows, gate_up_full, preferred_element_type=jnp.float32)
    units = gate_up_full.shape[1] // 2
    gate_part = projected[:, :units]
    up_part = projected[:, units:]
    sigmoid_gate = jax.nn.sigmoid(gate_part)
    silu_gate = gate_part * sigmoid_gate
    hidden = (silu_gate * up_part).astype(jnp.bfloat16)
    return (hidden, gate_part, up_part, sigmoid_gate, silu_gate)


def weight_blocks(grad_rows, hidden):
    product = lax.dot_general(
        grad_rows, hidden, (((0,), (0,)), ((), ())), preferred_element_type=jnp.float32
    )
    parts = lax.axis_size("dp")
    blocks = (product * loss_scale).astype(jnp.bfloat16)
    return blocks.reshape(parts, blocks.shape[0] // parts, blocks.shape[1])


def shards(tokens, out_grad, routing, gate_probs, gate_up_weight, down_weight):
    peer_count = lax.axis_size("expert")
    local_count = gate_up_weight.shape[0]
    expert_count = peer_count * local_count
    tok_rows = tokens.shape[0]
    top_count = routing.shape[1]
    model_width = tokens.shape[1]
    capacity = max(2, 9 * tok_rows * top_count // (8 * expert_count))
    pair_count = tok_rows * top_count
    slot_count = expert_count * capacity
    flat_ids = routing.reshape(pair_count)
    onehot = (flat_ids[:, None] == jnp.arange(expert_count, dtype=jnp.int32)[None, :]).astype(
        jnp.int32
    )
    slot_rank = jnp.sum((jnp.cumsum(onehot, 0) - onehot) * onehot, 1)
    slot_of_pair = flat_ids * capacity + slot_rank
    pair_index = jnp.arange(pair_count, dtype=jnp.int32)
    matches = slot_of_pair[None, :] == jnp.arange(slot_count, dtype=jnp.int32)[:, None]
    filled = jnp.any(matches, axis=1)
    source = jnp.sum(jnp.where(matches, pair_index[None, :], 0), axis=1)
    token_of_slot = source // top_count
    probs_flat = gate_probs.reshape(pair_count)
    weight_slot = jnp.where(filled, probs_flat[source], jnp.float32(0.0))
    send_rows = jnp.where(filled[:, None], tokens[token_of_slot], jnp.zeros((), jnp.bfloat16))
    send_grad = (weight_slot[:, None] * out_grad[token_of_slot].astype(jnp.float32)).astype(
        jnp.bfloat16
    )
    block_shape = (peer_count, local_count * capacity, 2 * model_width)
    send_both = jnp.concatenate([send_rows, send_grad], axis=1).reshape(block_shape)
    gate_width = gate_up_weight.shape[2]
    joined = jnp.concatenate([gate_up_weight[0], down_weight[0]], axis=1)
    recv_both, gathered = exchange(send_both, joined, True, 0)
    recv_both = recv_both.reshape(-1, 2 * model_width)
    expert_rows = recv_both[:, :model_width]
    grad_rows = recv_both[:, model_width:]
    full_joined = gathered.reshape(-1, joined.shape[1])
    full_gate_up = full_joined[:, :gate_width]
    full_down = full_joined[:, gate_width:]
    hidden, gate_part, up_part, sigmoid_gate, silu_gate = swiglu_forward(expert_rows, full_gate_up)
    produced = lax.dot_general(
        hidden, full_down, (((1,), (1,)), ((), ())), preferred_element_type=jnp.float32
    )
    down_parts = weight_blocks(grad_rows, hidden)
    hidden_grad = jnp.dot(grad_rows, full_down, preferred_element_type=jnp.float32)
    pre_grad = jnp.concatenate(
        [
            hidden_grad * up_part * sigmoid_gate * (1.0 + gate_part * (1.0 - sigmoid_gate)),
            hidden_grad * silu_gate,
        ],
        axis=1,
    ).astype(jnp.bfloat16)
    input_grad = lax.dot_general(
        pre_grad, full_gate_up, (((1,), (1,)), ((), ())), preferred_element_type=jnp.float32
    )
    back_both = jnp.concatenate(
        [produced.astype(jnp.bfloat16), input_grad.astype(jnp.bfloat16)], axis=1
    ).reshape(block_shape)
    returned, down_recv = exchange(back_both, down_parts, False, 1)
    returned = returned.reshape(slot_count, 2 * model_width)
    out_pairs = returned[:, :model_width][slot_of_pair]
    grad_pairs = returned[:, model_width:][slot_of_pair]
    weighted = probs_flat[:, None] * out_pairs.astype(jnp.float32)
    mixed = jnp.sum(weighted.reshape(tok_rows, top_count, model_width), axis=1).astype(jnp.bfloat16)
    token_grad = jnp.sum(
        grad_pairs.astype(jnp.float32).reshape(tok_rows, top_count, model_width), axis=1
    ).astype(jnp.bfloat16)
    down_grad = jnp.sum(down_recv.astype(jnp.float32), axis=0)[None].astype(jnp.bfloat16)
    return (mixed, token_grad, down_grad)


def solution(mesh):
    in_specs = (
        P(("dp", "expert"), None),
        P(("dp", "expert"), None),
        P(("dp", "expert"), None),
        P(("dp", "expert"), None),
        P("expert", "dp", None),
        P("expert", "dp", None),
    )
    out_specs = (P(("dp", "expert"), None), P(("dp", "expert"), None), P("expert", "dp", None))
    return jax.shard_map(shards, mesh=mesh, in_specs=in_specs, out_specs=out_specs, check_vma=False)
```

```python
import functools

import jax
import jax.numpy as jnp
from jax import lax
from jax.experimental import pallas as pl
from jax.experimental.pallas import tpu as pltpu
from jax.sharding import PartitionSpec as P

MESH = pl.DeviceIdType.MESH

loss_scale = 0.03125


def exchange_kernel(n_dp, n_ex, n_lo, bcast, ex_send, dp_send, ex_recv, dp_recv, send_sems, recv_sems, own_sems):
    q = lax.axis_index("dp")
    p = lax.axis_index("expert")
    n_hi = n_dp // n_lo
    row = q // n_lo
    lo = q % n_lo
    barrier = pltpu.get_barrier_semaphore()

    def greet_ex(k, c):
        pl.semaphore_signal(barrier, 1, device_id=(q, lax.rem(p + k, n_ex)), device_id_type=MESH)
        return c

    def greet_dp(k, c):
        pl.semaphore_signal(barrier, 1, device_id=(lax.rem(q + k, n_dp), p), device_id_type=MESH)
        return c

    lax.fori_loop(1, n_ex, greet_ex, 0)
    lax.fori_loop(1, n_dp, greet_dp, 0)
    pl.semaphore_wait(barrier, n_ex + n_dp - 2)

    def ex_copy(j, slot):
        return pltpu.make_async_remote_copy(
            src_ref=ex_send.at[j], dst_ref=ex_recv.at[slot], send_sem=send_sems.at[j],
            recv_sem=recv_sems.at[slot], device_id=(q, j), device_id_type=MESH)

    def dp_copy(i, slot):
        src = dp_send if bcast else dp_send.at[i]
        return pltpu.make_async_remote_copy(
            src_ref=src, dst_ref=dp_recv.at[slot], send_sem=send_sems.at[n_ex + i],
            recv_sem=recv_sems.at[n_ex + slot], device_id=(i, p), device_id_type=MESH)

    def row_copy(r, slot_row, k):
        rows = pl.ds(pl.multiple_of(slot_row * n_lo, n_lo), n_lo)
        return pltpu.make_async_remote_copy(
            src_ref=dp_recv.at[rows], dst_ref=dp_recv.at[rows],
            send_sem=send_sems.at[n_ex + n_dp + k], recv_sem=recv_sems.at[n_ex + n_dp + slot_row],
            device_id=(r * n_lo + lo, p), device_id_type=MESH)

    def send_ex(k, c):
        ex_copy(lax.rem(p + k, n_ex), p).start()
        return c

    def send_dp(k, c):
        dp_copy(lax.rem(q + k, n_dp), q).start()
        return c

    def send_lo(k, c):
        dp_copy(row * n_lo + lax.rem(lo + k, n_lo), q).start()
        return c

    own_dp = pltpu.make_async_copy(dp_send if bcast else dp_send.at[q], dp_recv.at[q], own_sems.at[1])
    if bcast:
        lax.fori_loop(1, n_lo, send_lo, 0)
    else:
        lax.fori_loop(1, n_dp, send_dp, 0)
    own_dp.start()
    lax.fori_loop(1, n_ex, send_ex, 0)
    own_ex = pltpu.make_async_copy(ex_send.at[p], ex_recv.at[p], own_sems.at[0])
    own_ex.start()

    def wait_ex(k, c):
        j = lax.rem(p + k, n_ex)
        ex_copy(j, p).wait_send()
        ex_copy(j, j).wait_recv()
        return c

    def wait_dp(k, c):
        i = lax.rem(q + k, n_dp)
        dp_copy(i, q).wait_send()
        dp_copy(i, i).wait_recv()
        return c

    def wait_lo(k, c):
        i = row * n_lo + lax.rem(lo + k, n_lo)
        dp_copy(i, q).wait_send()
        dp_copy(i, i).wait_recv()
        return c

    def send_hi(k, c):
        row_copy(lax.rem(row + k, n_hi), row, k).start()
        return c

    def wait_hi(k, c):
        r = lax.rem(row + k, n_hi)
        row_copy(r, row, k).wait_send()
        row_copy(r, r, k).wait_recv()
        return c

    if bcast:
        lax.fori_loop(1, n_lo, wait_lo, 0)
        own_dp.wait()
        lax.fori_loop(1, n_hi, send_hi, 0)
        lax.fori_loop(1, n_ex, wait_ex, 0)
        lax.fori_loop(1, n_hi, wait_hi, 0)
    else:
        lax.fori_loop(1, n_ex, wait_ex, 0)
        lax.fori_loop(1, n_dp, wait_dp, 0)
        own_dp.wait()
    own_ex.wait()


def exchange(ex_send, dp_send, bcast, cid):
    n_dp = lax.axis_size("dp")
    n_ex = lax.axis_size("expert")
    dp_block = dp_send.shape if bcast else dp_send.shape[1:]
    n_lo = 4 if n_dp % 4 == 0 else n_dp
    return pl.pallas_call(
        functools.partial(exchange_kernel, n_dp, n_ex, n_lo, bcast),
        out_shape=(
            jax.ShapeDtypeStruct(ex_send.shape, ex_send.dtype),
            jax.ShapeDtypeStruct((n_dp,) + tuple(dp_block), dp_send.dtype),
        ),
        in_specs=[pl.BlockSpec(memory_space=pl.ANY)] * 2,
        out_specs=(pl.BlockSpec(memory_space=pl.ANY), pl.BlockSpec(memory_space=pl.ANY)),
        scratch_shapes=[
            pltpu.SemaphoreType.DMA((n_ex + n_dp + n_dp,)),
            pltpu.SemaphoreType.DMA((n_ex + n_dp + n_dp,)),
            pltpu.SemaphoreType.DMA((2,)),
        ],
        compiler_params=pltpu.CompilerParams(collective_id=cid, has_side_effects=True),
    )(ex_send, dp_send)


def swiglu_forward(expert_rows, gate_up_full):
    projected = jnp.dot(expert_rows, gate_up_full, preferred_element_type=jnp.float32)
    units = gate_up_full.shape[1] // 2
    gate_part = projected[:, :units]
    up_part = projected[:, units:]
    sigmoid_gate = jax.nn.sigmoid(gate_part)
    silu_gate = gate_part * sigmoid_gate
    hidden = (silu_gate * up_part).astype(jnp.bfloat16)
    return (hidden, gate_part, up_part, sigmoid_gate, silu_gate)


def weight_blocks(grad_rows, hidden):
    product = lax.dot_general(
        grad_rows, hidden, (((0,), (0,)), ((), ())), preferred_element_type=jnp.float32
    )
    parts = lax.axis_size("dp")
    blocks = (product * loss_scale).astype(jnp.bfloat16)
    return blocks.reshape(parts, blocks.shape[0] // parts, blocks.shape[1])


def shards(tokens, out_grad, routing, gate_probs, gate_up_weight, down_weight):
    peer_count = lax.axis_size("expert")
    local_count = gate_up_weight.shape[0]
    expert_count = peer_count * local_count
    tok_rows = tokens.shape[0]
    top_count = routing.shape[1]
    model_width = tokens.shape[1]
    capacity = max(2, 9 * tok_rows * top_count // (8 * expert_count))
    pair_count = tok_rows * top_count
    slot_count = expert_count * capacity
    flat_ids = routing.reshape(pair_count)
    onehot = (flat_ids[:, None] == jnp.arange(expert_count, dtype=jnp.int32)[None, :]).astype(
        jnp.int32
    )
    slot_rank = jnp.sum((jnp.cumsum(onehot, 0) - onehot) * onehot, 1)
    slot_of_pair = flat_ids * capacity + slot_rank
    pair_index = jnp.arange(pair_count, dtype=jnp.int32)
    matches = slot_of_pair[None, :] == jnp.arange(slot_count, dtype=jnp.int32)[:, None]
    filled = jnp.any(matches, axis=1)
    source = jnp.sum(jnp.where(matches, pair_index[None, :], 0), axis=1)
    token_of_slot = source // top_count
    probs_flat = gate_probs.reshape(pair_count)
    weight_slot = jnp.where(filled, probs_flat[source], jnp.float32(0.0))
    send_rows = jnp.where(filled[:, None], tokens[token_of_slot], jnp.zeros((), jnp.bfloat16))
    send_grad = (weight_slot[:, None] * out_grad[token_of_slot].astype(jnp.float32)).astype(
        jnp.bfloat16
    )
    block_shape = (peer_count, local_count * capacity, 2 * model_width)
    send_both = jnp.concatenate([send_rows, send_grad], axis=1).reshape(block_shape)
    gate_width = gate_up_weight.shape[2]
    joined = jnp.concatenate([gate_up_weight[0], down_weight[0]], axis=1)
    recv_both, gathered = exchange(send_both, joined, True, 0)
    recv_both = recv_both.reshape(-1, 2 * model_width)
    expert_rows = recv_both[:, :model_width]
    grad_rows = recv_both[:, model_width:]
    full_joined = gathered.reshape(-1, joined.shape[1])
    full_gate_up = full_joined[:, :gate_width]
    full_down = full_joined[:, gate_width:]
    hidden, gate_part, up_part, sigmoid_gate, silu_gate = swiglu_forward(expert_rows, full_gate_up)
    produced = lax.dot_general(
        hidden, full_down, (((1,), (1,)), ((), ())), preferred_element_type=jnp.float32
    )
    down_parts = weight_blocks(grad_rows, hidden)
    hidden_grad = jnp.dot(grad_rows, full_down, preferred_element_type=jnp.float32)
    pre_grad = jnp.concatenate(
        [
            hidden_grad * up_part * sigmoid_gate * (1.0 + gate_part * (1.0 - sigmoid_gate)),
            hidden_grad * silu_gate,
        ],
        axis=1,
    ).astype(jnp.bfloat16)
    input_grad = lax.dot_general(
        pre_grad, full_gate_up, (((1,), (1,)), ((), ())), preferred_element_type=jnp.float32
    )
    back_both = jnp.concatenate(
        [produced.astype(jnp.bfloat16), input_grad.astype(jnp.bfloat16)], axis=1
    ).reshape(block_shape)
    returned, down_recv = exchange(back_both, down_parts, False, 1)
    returned = returned.reshape(slot_count, 2 * model_width)
    out_pairs = returned[:, :model_width][slot_of_pair]
    grad_pairs = returned[:, model_width:][slot_of_pair]
    weighted = probs_flat[:, None] * out_pairs.astype(jnp.float32)
    mixed = jnp.sum(weighted.reshape(tok_rows, top_count, model_width), axis=1).astype(jnp.bfloat16)
    token_grad = jnp.sum(
        grad_pairs.astype(jnp.float32).reshape(tok_rows, top_count, model_width), axis=1
    ).astype(jnp.bfloat16)
    down_grad = jnp.sum(down_recv.astype(jnp.float32), axis=0)[None].astype(jnp.bfloat16)
    return (mixed, token_grad, down_grad)


def solution(mesh):
    in_specs = (
        P(("dp", "expert"), None),
        P(("dp", "expert"), None),
        P(("dp", "expert"), None),
        P(("dp", "expert"), None),
        P("expert", "dp", None),
        P("expert", "dp", None),
    )
    out_specs = (P(("dp", "expert"), None), P(("dp", "expert"), None), P("expert", "dp", None))
    return jax.shard_map(shards, mesh=mesh, in_specs=in_specs, out_specs=out_specs, check_vma=False)
```

```python
import functools

import jax
import jax.numpy as jnp
from jax import lax
from jax.experimental import pallas as pl
from jax.experimental.pallas import tpu as pltpu
from jax.sharding import PartitionSpec as P

MESH = pl.DeviceIdType.MESH

loss_scale = 0.03125


def exchange_kernel(n_dp, n_ex, n_lo, bcast, ex_send, dp_send, ex_recv, dp_recv, send_sems, recv_sems, own_sems):
    q = lax.axis_index("dp")
    p = lax.axis_index("expert")
    n_hi = n_dp // n_lo
    row = q // n_lo
    lo = q % n_lo
    barrier = pltpu.get_barrier_semaphore()
    far = n_lo == 4 and n_ex % 8 == 0

    def peer_q(j):
        if not far:
            return q
        gap = lax.rem(j // 2 - p // 2 + 8 * n_ex, 4)
        return q + (gap // 2) * (1 - gap % 2) * (3 - 2 * lo)

    def greet_ex(k, c):
        j = lax.rem(p + k, n_ex)
        pl.semaphore_signal(barrier, 1, device_id=(peer_q(j), j), device_id_type=MESH)
        return c

    def greet_dp(k, c):
        pl.semaphore_signal(barrier, 1, device_id=(lax.rem(q + k, n_dp), p), device_id_type=MESH)
        return c

    lax.fori_loop(1, n_ex, greet_ex, 0)
    lax.fori_loop(1, n_dp, greet_dp, 0)
    pl.semaphore_wait(barrier, n_ex + n_dp - 2)

    def ex_copy(j, slot):
        return pltpu.make_async_remote_copy(
            src_ref=ex_send.at[j], dst_ref=ex_recv.at[slot], send_sem=send_sems.at[j],
            recv_sem=recv_sems.at[slot], device_id=(peer_q(j), j), device_id_type=MESH)

    def dp_copy(i, slot):
        src = dp_send if bcast else dp_send.at[i]
        return pltpu.make_async_remote_copy(
            src_ref=src, dst_ref=dp_recv.at[slot], send_sem=send_sems.at[n_ex + i],
            recv_sem=recv_sems.at[n_ex + slot], device_id=(i, p), device_id_type=MESH)

    def row_copy(r, slot_row, k):
        rows = pl.ds(pl.multiple_of(slot_row * n_lo, n_lo), n_lo)
        return pltpu.make_async_remote_copy(
            src_ref=dp_recv.at[rows], dst_ref=dp_recv.at[rows],
            send_sem=send_sems.at[n_ex + n_dp + k], recv_sem=recv_sems.at[n_ex + n_dp + slot_row],
            device_id=(r * n_lo + lo, p), device_id_type=MESH)

    def send_ex(k, c):
        ex_copy(lax.rem(p + k, n_ex), p).start()
        return c

    def send_dp(k, c):
        dp_copy(lax.rem(q + k, n_dp), q).start()
        return c

    def send_lo(k, c):
        dp_copy(row * n_lo + lax.rem(lo + k, n_lo), q).start()
        return c

    own_dp = pltpu.make_async_copy(dp_send if bcast else dp_send.at[q], dp_recv.at[q], own_sems.at[1])
    if bcast:
        lax.fori_loop(1, n_lo, send_lo, 0)
    else:
        lax.fori_loop(1, n_dp, send_dp, 0)
    own_dp.start()
    lax.fori_loop(1, n_ex, send_ex, 0)
    own_ex = pltpu.make_async_copy(ex_send.at[p], ex_recv.at[p], own_sems.at[0])
    own_ex.start()

    def wait_ex(k, c):
        j = lax.rem(p + k, n_ex)
        ex_copy(j, p).wait_send()
        ex_copy(j, j).wait_recv()
        return c

    def wait_dp(k, c):
        i = lax.rem(q + k, n_dp)
        dp_copy(i, q).wait_send()
        dp_copy(i, i).wait_recv()
        return c

    def wait_lo(k, c):
        i = row * n_lo + lax.rem(lo + k, n_lo)
        dp_copy(i, q).wait_send()
        dp_copy(i, i).wait_recv()
        return c

    def send_hi(k, c):
        row_copy(lax.rem(row + k, n_hi), row, k).start()
        return c

    def wait_hi(k, c):
        r = lax.rem(row + k, n_hi)
        row_copy(r, row, k).wait_send()
        row_copy(r, r, k).wait_recv()
        return c

    if bcast:
        lax.fori_loop(1, n_lo, wait_lo, 0)
        own_dp.wait()
        lax.fori_loop(1, n_hi, send_hi, 0)
        lax.fori_loop(1, n_ex, wait_ex, 0)
        lax.fori_loop(1, n_hi, wait_hi, 0)
    else:
        lax.fori_loop(1, n_ex, wait_ex, 0)
        lax.fori_loop(1, n_dp, wait_dp, 0)
        own_dp.wait()
    own_ex.wait()


def exchange(ex_send, dp_send, bcast, cid):
    n_dp = lax.axis_size("dp")
    n_ex = lax.axis_size("expert")
    dp_block = dp_send.shape if bcast else dp_send.shape[1:]
    n_lo = 4 if n_dp % 4 == 0 else n_dp
    return pl.pallas_call(
        functools.partial(exchange_kernel, n_dp, n_ex, n_lo, bcast),
        out_shape=(
            jax.ShapeDtypeStruct(ex_send.shape, ex_send.dtype),
            jax.ShapeDtypeStruct((n_dp,) + tuple(dp_block), dp_send.dtype),
        ),
        in_specs=[pl.BlockSpec(memory_space=pl.ANY)] * 2,
        out_specs=(pl.BlockSpec(memory_space=pl.ANY), pl.BlockSpec(memory_space=pl.ANY)),
        scratch_shapes=[
            pltpu.SemaphoreType.DMA((n_ex + n_dp + n_dp,)),
            pltpu.SemaphoreType.DMA((n_ex + n_dp + n_dp,)),
            pltpu.SemaphoreType.DMA((2,)),
        ],
        compiler_params=pltpu.CompilerParams(collective_id=cid, has_side_effects=True),
    )(ex_send, dp_send)


def swiglu_forward(expert_rows, gate_up_full):
    projected = jnp.dot(expert_rows, gate_up_full, preferred_element_type=jnp.float32)
    units = gate_up_full.shape[1] // 2
    gate_part = projected[:, :units]
    up_part = projected[:, units:]
    sigmoid_gate = jax.nn.sigmoid(gate_part)
    silu_gate = gate_part * sigmoid_gate
    hidden = (silu_gate * up_part).astype(jnp.bfloat16)
    return (hidden, gate_part, up_part, sigmoid_gate, silu_gate)


def weight_blocks(grad_rows, hidden):
    product = lax.dot_general(
        grad_rows, hidden, (((0,), (0,)), ((), ())), preferred_element_type=jnp.float32
    )
    parts = lax.axis_size("dp")
    blocks = (product * loss_scale).astype(jnp.bfloat16)
    return blocks.reshape(parts, blocks.shape[0] // parts, blocks.shape[1])


def shards(tokens, out_grad, routing, gate_probs, gate_up_weight, down_weight):
    peer_count = lax.axis_size("expert")
    local_count = gate_up_weight.shape[0]
    expert_count = peer_count * local_count
    tok_rows = tokens.shape[0]
    top_count = routing.shape[1]
    model_width = tokens.shape[1]
    capacity = max(2, 9 * tok_rows * top_count // (8 * expert_count))
    pair_count = tok_rows * top_count
    slot_count = expert_count * capacity
    flat_ids = routing.reshape(pair_count)
    onehot = (flat_ids[:, None] == jnp.arange(expert_count, dtype=jnp.int32)[None, :]).astype(
        jnp.int32
    )
    slot_rank = jnp.sum((jnp.cumsum(onehot, 0) - onehot) * onehot, 1)
    slot_of_pair = flat_ids * capacity + slot_rank
    pair_index = jnp.arange(pair_count, dtype=jnp.int32)
    matches = slot_of_pair[None, :] == jnp.arange(slot_count, dtype=jnp.int32)[:, None]
    filled = jnp.any(matches, axis=1)
    source = jnp.sum(jnp.where(matches, pair_index[None, :], 0), axis=1)
    token_of_slot = source // top_count
    probs_flat = gate_probs.reshape(pair_count)
    weight_slot = jnp.where(filled, probs_flat[source], jnp.float32(0.0))
    send_rows = jnp.where(filled[:, None], tokens[token_of_slot], jnp.zeros((), jnp.bfloat16))
    send_grad = (weight_slot[:, None] * out_grad[token_of_slot].astype(jnp.float32)).astype(
        jnp.bfloat16
    )
    block_shape = (peer_count, local_count * capacity, 2 * model_width)
    send_both = jnp.concatenate([send_rows, send_grad], axis=1).reshape(block_shape)
    gate_width = gate_up_weight.shape[2]
    joined = jnp.concatenate([gate_up_weight[0], down_weight[0]], axis=1)
    recv_both, gathered = exchange(send_both, joined, True, 0)
    recv_both = recv_both.reshape(-1, 2 * model_width)
    expert_rows = recv_both[:, :model_width]
    grad_rows = recv_both[:, model_width:]
    full_joined = gathered.reshape(-1, joined.shape[1])
    full_gate_up = full_joined[:, :gate_width]
    full_down = full_joined[:, gate_width:]
    hidden, gate_part, up_part, sigmoid_gate, silu_gate = swiglu_forward(expert_rows, full_gate_up)
    produced = lax.dot_general(
        hidden, full_down, (((1,), (1,)), ((), ())), preferred_element_type=jnp.float32
    )
    down_parts = weight_blocks(grad_rows, hidden)
    hidden_grad = jnp.dot(grad_rows, full_down, preferred_element_type=jnp.float32)
    pre_grad = jnp.concatenate(
        [
            hidden_grad * up_part * sigmoid_gate * (1.0 + gate_part * (1.0 - sigmoid_gate)),
            hidden_grad * silu_gate,
        ],
        axis=1,
    ).astype(jnp.bfloat16)
    input_grad = lax.dot_general(
        pre_grad, full_gate_up, (((1,), (1,)), ((), ())), preferred_element_type=jnp.float32
    )
    back_both = jnp.concatenate(
        [produced.astype(jnp.bfloat16), input_grad.astype(jnp.bfloat16)], axis=1
    ).reshape(block_shape)
    returned, down_recv = exchange(back_both, down_parts, False, 1)
    returned = returned.reshape(slot_count, 2 * model_width)
    out_pairs = returned[:, :model_width][slot_of_pair]
    grad_pairs = returned[:, model_width:][slot_of_pair]
    weighted = probs_flat[:, None] * out_pairs.astype(jnp.float32)
    mixed = jnp.sum(weighted.reshape(tok_rows, top_count, model_width), axis=1).astype(jnp.bfloat16)
    token_grad = jnp.sum(
        grad_pairs.astype(jnp.float32).reshape(tok_rows, top_count, model_width), axis=1
    ).astype(jnp.bfloat16)
    down_grad = jnp.sum(down_recv.astype(jnp.float32), axis=0)[None].astype(jnp.bfloat16)
    return (mixed, token_grad, down_grad)


def solution(mesh):
    in_specs = (
        P(("dp", "expert"), None),
        P(("dp", "expert"), None),
        P(("dp", "expert"), None),
        P(("dp", "expert"), None),
        P("expert", "dp", None),
        P("expert", "dp", None),
    )
    out_specs = (P(("dp", "expert"), None), P(("dp", "expert"), None), P("expert", "dp", None))
    return jax.shard_map(shards, mesh=mesh, in_specs=in_specs, out_specs=out_specs, check_vma=False)
```

```python
import functools

import jax
import jax.numpy as jnp
from jax import lax
from jax.experimental import pallas as pl
from jax.experimental.pallas import tpu as pltpu
from jax.sharding import PartitionSpec as P

MESH = pl.DeviceIdType.MESH

loss_scale = 0.03125


def exchange_kernel(n_dp, n_ex, n_lo, bcast, ex_send, dp_send, ex_recv, dp_recv, send_sems, recv_sems, own_sems):
    q = lax.axis_index("dp")
    p = lax.axis_index("expert")
    n_hi = n_dp // n_lo
    row = q // n_lo
    lo = q % n_lo
    barrier = pltpu.get_barrier_semaphore()
    far = n_lo == 4 and n_ex % 8 == 0

    def peer_q(j):
        if not far:
            return q
        gap = lax.rem(j // 2 - p // 2 + 8 * n_ex, 4)
        return q + (gap // 2) * (1 - gap % 2) * (3 - 2 * lo)

    def greet_ex(k, c):
        j = lax.rem(p + k, n_ex)
        pl.semaphore_signal(barrier, 1, device_id=(peer_q(j), j), device_id_type=MESH)
        return c

    def greet_dp(k, c):
        pl.semaphore_signal(barrier, 1, device_id=(lax.rem(q + k, n_dp), p), device_id_type=MESH)
        return c

    lax.fori_loop(1, n_ex, greet_ex, 0)
    lax.fori_loop(1, n_dp, greet_dp, 0)
    pl.semaphore_wait(barrier, n_ex + n_dp - 2)

    def ex_copy(j, slot):
        return pltpu.make_async_remote_copy(
            src_ref=ex_send.at[j], dst_ref=ex_recv.at[slot], send_sem=send_sems.at[j],
            recv_sem=recv_sems.at[slot], device_id=(peer_q(j), j), device_id_type=MESH)

    def dp_copy(i, slot):
        src = dp_send if bcast else dp_send.at[i]
        return pltpu.make_async_remote_copy(
            src_ref=src, dst_ref=dp_recv.at[slot], send_sem=send_sems.at[n_ex + i],
            recv_sem=recv_sems.at[n_ex + slot], device_id=(i, p), device_id_type=MESH)

    def row_copy(r, slot_row, k):
        rows = pl.ds(pl.multiple_of(slot_row * n_lo, n_lo), n_lo)
        return pltpu.make_async_remote_copy(
            src_ref=dp_recv.at[rows], dst_ref=dp_recv.at[rows],
            send_sem=send_sems.at[n_ex + n_dp + k], recv_sem=recv_sems.at[n_ex + n_dp + slot_row],
            device_id=(r * n_lo + lo, p), device_id_type=MESH)

    def send_ex(k, c):
        ex_copy(lax.rem(p + k, n_ex), p).start()
        return c

    def send_dp(k, c):
        dp_copy(lax.rem(q + k, n_dp), q).start()
        return c

    def send_lo(k, c):
        dp_copy(row * n_lo + lax.rem(lo + k, n_lo), q).start()
        return c

    own_dp = pltpu.make_async_copy(dp_send if bcast else dp_send.at[q], dp_recv.at[q], own_sems.at[1])
    if bcast:
        lax.fori_loop(1, n_lo, send_lo, 0)
    else:
        lax.fori_loop(1, n_dp, send_dp, 0)
    own_dp.start()
    lax.fori_loop(1, n_ex, send_ex, 0)
    own_ex = pltpu.make_async_copy(ex_send.at[p], ex_recv.at[p], own_sems.at[0])
    own_ex.start()

    def wait_ex(k, c):
        j = lax.rem(p + k, n_ex)
        ex_copy(j, p).wait_send()
        ex_copy(j, j).wait_recv()
        return c

    def wait_dp(k, c):
        i = lax.rem(q + k, n_dp)
        dp_copy(i, q).wait_send()
        dp_copy(i, i).wait_recv()
        return c

    def wait_lo(k, c):
        i = row * n_lo + lax.rem(lo + k, n_lo)
        dp_copy(i, q).wait_send()
        dp_copy(i, i).wait_recv()
        return c

    def send_hi(k, c):
        row_copy(lax.rem(row + k, n_hi), row, k).start()
        return c

    def wait_hi(k, c):
        r = lax.rem(row + k, n_hi)
        row_copy(r, row, k).wait_send()
        row_copy(r, r, k).wait_recv()
        return c

    if bcast:
        lax.fori_loop(1, n_lo, wait_lo, 0)
        own_dp.wait()
        lax.fori_loop(1, n_hi, send_hi, 0)
        lax.fori_loop(1, n_ex, wait_ex, 0)
        lax.fori_loop(1, n_hi, wait_hi, 0)
    else:
        lax.fori_loop(1, n_ex, wait_ex, 0)
        lax.fori_loop(1, n_dp, wait_dp, 0)
        own_dp.wait()
    own_ex.wait()


def exchange(ex_send, dp_send, bcast, cid):
    n_dp = lax.axis_size("dp")
    n_ex = lax.axis_size("expert")
    dp_block = dp_send.shape if bcast else dp_send.shape[1:]
    n_lo = 4 if n_dp % 4 == 0 else n_dp
    return pl.pallas_call(
        functools.partial(exchange_kernel, n_dp, n_ex, n_lo, bcast),
        out_shape=(
            jax.ShapeDtypeStruct(ex_send.shape, ex_send.dtype),
            jax.ShapeDtypeStruct((n_dp,) + tuple(dp_block), dp_send.dtype),
        ),
        in_specs=[pl.BlockSpec(memory_space=pl.ANY)] * 2,
        out_specs=(pl.BlockSpec(memory_space=pl.ANY), pl.BlockSpec(memory_space=pl.ANY)),
        scratch_shapes=[
            pltpu.SemaphoreType.DMA((n_ex + n_dp + n_dp,)),
            pltpu.SemaphoreType.DMA((n_ex + n_dp + n_dp,)),
            pltpu.SemaphoreType.DMA((2,)),
        ],
        compiler_params=pltpu.CompilerParams(collective_id=cid, has_side_effects=True),
    )(ex_send, dp_send)


def swiglu_forward(expert_rows, gate_up_full):
    projected = jnp.dot(expert_rows, gate_up_full, preferred_element_type=jnp.float32)
    units = gate_up_full.shape[1] // 2
    gate_part = projected[:, :units]
    up_part = projected[:, units:]
    sigmoid_gate = jax.nn.sigmoid(gate_part)
    silu_gate = gate_part * sigmoid_gate
    hidden = (silu_gate * up_part).astype(jnp.bfloat16)
    return (hidden, gate_part, up_part, sigmoid_gate, silu_gate)


def weight_blocks(grad_rows, hidden):
    product = lax.dot_general(
        grad_rows, hidden, (((0,), (0,)), ((), ())), preferred_element_type=jnp.float32
    )
    parts = lax.axis_size("dp")
    blocks = (product * loss_scale).astype(jnp.bfloat16)
    return blocks.reshape(parts, blocks.shape[0] // parts, blocks.shape[1])


def shards(tokens, out_grad, routing, gate_probs, gate_up_weight, down_weight):
    peer_count = lax.axis_size("expert")
    local_count = gate_up_weight.shape[0]
    expert_count = peer_count * local_count
    tok_rows = tokens.shape[0]
    top_count = routing.shape[1]
    model_width = tokens.shape[1]
    capacity = max(2, 9 * tok_rows * top_count // (8 * expert_count))
    pair_count = tok_rows * top_count
    slot_count = expert_count * capacity
    flat_ids = routing.reshape(pair_count)
    onehot = (flat_ids[:, None] == jnp.arange(expert_count, dtype=jnp.int32)[None, :]).astype(
        jnp.int32
    )
    slot_rank = jnp.sum((jnp.cumsum(onehot, 0) - onehot) * onehot, 1)
    slot_of_pair = flat_ids * capacity + slot_rank
    pair_index = jnp.arange(pair_count, dtype=jnp.int32)
    matches = slot_of_pair[None, :] == jnp.arange(slot_count, dtype=jnp.int32)[:, None]
    filled = jnp.any(matches, axis=1)
    source = jnp.sum(jnp.where(matches, pair_index[None, :], 0), axis=1)
    token_of_slot = source // top_count
    probs_flat = gate_probs.reshape(pair_count)
    weight_slot = jnp.where(filled, probs_flat[source], jnp.float32(0.0))
    send_rows = jnp.where(filled[:, None], tokens[token_of_slot], jnp.zeros((), jnp.bfloat16))
    send_grad = (weight_slot[:, None] * out_grad[token_of_slot].astype(jnp.float32)).astype(
        jnp.bfloat16
    )
    block_shape = (peer_count, local_count * capacity * 2 * model_width // 128, 128)
    send_both = jnp.concatenate([send_rows, send_grad], axis=1).reshape(block_shape)
    gate_width = gate_up_weight.shape[2]
    joined = jnp.concatenate([gate_up_weight[0], down_weight[0]], axis=1)
    recv_both, gathered = exchange(send_both, joined, True, 0)
    recv_both = recv_both.reshape(-1, 2 * model_width)
    expert_rows = recv_both[:, :model_width]
    grad_rows = recv_both[:, model_width:]
    full_joined = gathered.reshape(-1, joined.shape[1])
    full_gate_up = full_joined[:, :gate_width]
    full_down = full_joined[:, gate_width:]
    hidden, gate_part, up_part, sigmoid_gate, silu_gate = swiglu_forward(expert_rows, full_gate_up)
    produced = lax.dot_general(
        hidden, full_down, (((1,), (1,)), ((), ())), preferred_element_type=jnp.float32
    )
    down_parts = weight_blocks(grad_rows, hidden)
    hidden_grad = jnp.dot(grad_rows, full_down, preferred_element_type=jnp.float32)
    pre_grad = jnp.concatenate(
        [
            hidden_grad * up_part * sigmoid_gate * (1.0 + gate_part * (1.0 - sigmoid_gate)),
            hidden_grad * silu_gate,
        ],
        axis=1,
    ).astype(jnp.bfloat16)
    input_grad = lax.dot_general(
        pre_grad, full_gate_up, (((1,), (1,)), ((), ())), preferred_element_type=jnp.float32
    )
    back_both = jnp.concatenate(
        [produced.astype(jnp.bfloat16), input_grad.astype(jnp.bfloat16)], axis=1
    ).reshape(block_shape)
    returned, down_recv = exchange(back_both, down_parts, False, 1)
    returned = returned.reshape(slot_count, 2 * model_width)
    out_pairs = returned[:, :model_width][slot_of_pair]
    grad_pairs = returned[:, model_width:][slot_of_pair]
    weighted = probs_flat[:, None] * out_pairs.astype(jnp.float32)
    mixed = jnp.sum(weighted.reshape(tok_rows, top_count, model_width), axis=1).astype(jnp.bfloat16)
    token_grad = jnp.sum(
        grad_pairs.astype(jnp.float32).reshape(tok_rows, top_count, model_width), axis=1
    ).astype(jnp.bfloat16)
    down_grad = jnp.sum(down_recv.astype(jnp.float32), axis=0)[None].astype(jnp.bfloat16)
    return (mixed, token_grad, down_grad)


def solution(mesh):
    in_specs = (
        P(("dp", "expert"), None),
        P(("dp", "expert"), None),
        P(("dp", "expert"), None),
        P(("dp", "expert"), None),
        P("expert", "dp", None),
        P("expert", "dp", None),
    )
    out_specs = (P(("dp", "expert"), None), P(("dp", "expert"), None), P("expert", "dp", None))
    return jax.shard_map(shards, mesh=mesh, in_specs=in_specs, out_specs=out_specs, check_vma=False)
```

```python
import functools

import jax
import jax.numpy as jnp
from jax import lax
from jax.experimental import pallas as pl
from jax.experimental.pallas import tpu as pltpu
from jax.sharding import PartitionSpec as P

MESH = pl.DeviceIdType.MESH

loss_scale = 0.03125


def exchange_kernel(n_dp, n_ex, n_lo, bcast, ex_send, dp_send, ex_recv, dp_recv, send_sems, recv_sems, own_sems):
    q = lax.axis_index("dp")
    p = lax.axis_index("expert")
    n_hi = n_dp // n_lo
    row = q // n_lo
    lo = q % n_lo
    barrier = pltpu.get_barrier_semaphore()
    far = n_lo == 4 and n_ex % 8 == 0

    def peer_q(j):
        if not far:
            return q
        gap = lax.rem(j // 2 - p // 2 + 8 * n_ex, 4)
        return q + (gap // 2) * (1 - gap % 2) * (3 - 2 * lo)

    def greet_ex(k, c):
        j = lax.rem(p + k, n_ex)
        pl.semaphore_signal(barrier, 1, device_id=(peer_q(j), j), device_id_type=MESH)
        return c

    def greet_dp(k, c):
        pl.semaphore_signal(barrier, 1, device_id=(lax.rem(q + k, n_dp), p), device_id_type=MESH)
        return c

    lax.fori_loop(1, n_ex, greet_ex, 0)
    lax.fori_loop(1, n_dp, greet_dp, 0)
    pl.semaphore_wait(barrier, n_ex + n_dp - 2)

    def ex_copy(j, slot):
        return pltpu.make_async_remote_copy(
            src_ref=ex_send.at[j], dst_ref=ex_recv.at[slot], send_sem=send_sems.at[j],
            recv_sem=recv_sems.at[slot], device_id=(peer_q(j), j), device_id_type=MESH)

    def dp_copy(i, slot):
        src = dp_send if bcast else dp_send.at[i]
        return pltpu.make_async_remote_copy(
            src_ref=src, dst_ref=dp_recv.at[slot], send_sem=send_sems.at[n_ex + i],
            recv_sem=recv_sems.at[n_ex + slot], device_id=(i, p), device_id_type=MESH)

    def row_copy(r, slot_row, k):
        rows = pl.ds(pl.multiple_of(slot_row * n_lo, n_lo), n_lo)
        return pltpu.make_async_remote_copy(
            src_ref=dp_recv.at[rows], dst_ref=dp_recv.at[rows],
            send_sem=send_sems.at[n_ex + n_dp + k], recv_sem=recv_sems.at[n_ex + n_dp + slot_row],
            device_id=(r * n_lo + lo, p), device_id_type=MESH)

    def send_ex(k, c):
        ex_copy(lax.rem(p + k, n_ex), p).start()
        return c

    def send_dp(k, c):
        dp_copy(lax.rem(q + k, n_dp), q).start()
        return c

    def send_lo(k, c):
        dp_copy(row * n_lo + lax.rem(lo + k, n_lo), q).start()
        return c

    own_dp = pltpu.make_async_copy(dp_send if bcast else dp_send.at[q], dp_recv.at[q], own_sems.at[1])
    if bcast:
        lax.fori_loop(1, n_lo, send_lo, 0)
    else:
        lax.fori_loop(1, n_dp, send_dp, 0)
    own_dp.start()
    lax.fori_loop(1, n_ex, send_ex, 0)
    own_ex = pltpu.make_async_copy(ex_send.at[p], ex_recv.at[p], own_sems.at[0])
    own_ex.start()

    def wait_ex(k, c):
        j = lax.rem(p + k, n_ex)
        ex_copy(j, p).wait_send()
        ex_copy(j, j).wait_recv()
        return c

    def wait_dp(k, c):
        i = lax.rem(q + k, n_dp)
        dp_copy(i, q).wait_send()
        dp_copy(i, i).wait_recv()
        return c

    def wait_lo(k, c):
        i = row * n_lo + lax.rem(lo + k, n_lo)
        dp_copy(i, q).wait_send()
        dp_copy(i, i).wait_recv()
        return c

    def send_hi(k, c):
        row_copy(lax.rem(row + k, n_hi), row, k).start()
        return c

    def wait_hi(k, c):
        r = lax.rem(row + k, n_hi)
        row_copy(r, row, k).wait_send()
        row_copy(r, r, k).wait_recv()
        return c

    def fwd_copy(start, count, target_row, s_idx, r_idx):
        rows = dp_recv.at[pl.ds(start, count)]
        return pltpu.make_async_remote_copy(
            src_ref=rows, dst_ref=rows, send_sem=send_sems.at[n_ex + n_dp + s_idx],
            recv_sem=recv_sems.at[n_ex + n_dp + r_idx],
            device_id=(target_row * n_lo + lo, p), device_id_type=MESH)

    if bcast and n_hi == 4:
        half = n_lo // 2
        up = lax.rem(row + 1, 4)
        dn = lax.rem(row + 3, 4)
        far_row = lax.rem(row + 2, 4)
        lax.fori_loop(1, n_lo, wait_lo, 0)
        own_dp.wait()
        to_up = fwd_copy(row * n_lo, n_lo, up, 0, row)
        to_dn = fwd_copy(row * n_lo, n_lo, dn, 1, row)
        to_up.start()
        to_dn.start()
        fwd_copy(dn * n_lo, n_lo, dn, 0, dn).wait_recv()
        fwd_copy(up * n_lo, n_lo, up, 1, up).wait_recv()
        pass_up = fwd_copy(dn * n_lo, half, up, 2, 4)
        pass_dn = fwd_copy(up * n_lo + half, n_lo - half, dn, 3, 5)
        pass_up.start()
        pass_dn.start()
        lax.fori_loop(1, n_ex, wait_ex, 0)
        fwd_copy(far_row * n_lo, half, up, 2, 4).wait_recv()
        fwd_copy(far_row * n_lo + half, n_lo - half, dn, 3, 5).wait_recv()
        to_up.wait_send()
        to_dn.wait_send()
        pass_up.wait_send()
        pass_dn.wait_send()
    elif bcast:
        lax.fori_loop(1, n_lo, wait_lo, 0)
        own_dp.wait()
        lax.fori_loop(1, n_hi, send_hi, 0)
        lax.fori_loop(1, n_ex, wait_ex, 0)
        lax.fori_loop(1, n_hi, wait_hi, 0)
    else:
        lax.fori_loop(1, n_ex, wait_ex, 0)
        lax.fori_loop(1, n_dp, wait_dp, 0)
        own_dp.wait()
    own_ex.wait()


def exchange(ex_send, dp_send, bcast, cid):
    n_dp = lax.axis_size("dp")
    n_ex = lax.axis_size("expert")
    dp_block = dp_send.shape if bcast else dp_send.shape[1:]
    n_lo = 4 if n_dp % 4 == 0 else n_dp
    return pl.pallas_call(
        functools.partial(exchange_kernel, n_dp, n_ex, n_lo, bcast),
        out_shape=(
            jax.ShapeDtypeStruct(ex_send.shape, ex_send.dtype),
            jax.ShapeDtypeStruct((n_dp,) + tuple(dp_block), dp_send.dtype),
        ),
        in_specs=[pl.BlockSpec(memory_space=pl.ANY)] * 2,
        out_specs=(pl.BlockSpec(memory_space=pl.ANY), pl.BlockSpec(memory_space=pl.ANY)),
        scratch_shapes=[
            pltpu.SemaphoreType.DMA((n_ex + n_dp + n_dp,)),
            pltpu.SemaphoreType.DMA((n_ex + n_dp + n_dp,)),
            pltpu.SemaphoreType.DMA((2,)),
        ],
        compiler_params=pltpu.CompilerParams(collective_id=cid, has_side_effects=True),
    )(ex_send, dp_send)


def swiglu_forward(expert_rows, gate_up_full):
    projected = jnp.dot(expert_rows, gate_up_full, preferred_element_type=jnp.float32)
    units = gate_up_full.shape[1] // 2
    gate_part = projected[:, :units]
    up_part = projected[:, units:]
    sigmoid_gate = jax.nn.sigmoid(gate_part)
    silu_gate = gate_part * sigmoid_gate
    hidden = (silu_gate * up_part).astype(jnp.bfloat16)
    return (hidden, gate_part, up_part, sigmoid_gate, silu_gate)


def weight_blocks(grad_rows, hidden):
    product = lax.dot_general(
        grad_rows, hidden, (((0,), (0,)), ((), ())), preferred_element_type=jnp.float32
    )
    parts = lax.axis_size("dp")
    blocks = (product * loss_scale).astype(jnp.bfloat16)
    return blocks.reshape(parts, blocks.shape[0] // parts, blocks.shape[1])


def shards(tokens, out_grad, routing, gate_probs, gate_up_weight, down_weight):
    peer_count = lax.axis_size("expert")
    local_count = gate_up_weight.shape[0]
    expert_count = peer_count * local_count
    tok_rows = tokens.shape[0]
    top_count = routing.shape[1]
    model_width = tokens.shape[1]
    capacity = max(2, 9 * tok_rows * top_count // (8 * expert_count))
    pair_count = tok_rows * top_count
    slot_count = expert_count * capacity
    flat_ids = routing.reshape(pair_count)
    onehot = (flat_ids[:, None] == jnp.arange(expert_count, dtype=jnp.int32)[None, :]).astype(
        jnp.int32
    )
    slot_rank = jnp.sum((jnp.cumsum(onehot, 0) - onehot) * onehot, 1)
    slot_of_pair = flat_ids * capacity + slot_rank
    pair_index = jnp.arange(pair_count, dtype=jnp.int32)
    matches = slot_of_pair[None, :] == jnp.arange(slot_count, dtype=jnp.int32)[:, None]
    filled = jnp.any(matches, axis=1)
    source = jnp.sum(jnp.where(matches, pair_index[None, :], 0), axis=1)
    token_of_slot = source // top_count
    probs_flat = gate_probs.reshape(pair_count)
    weight_slot = jnp.where(filled, probs_flat[source], jnp.float32(0.0))
    send_rows = jnp.where(filled[:, None], tokens[token_of_slot], jnp.zeros((), jnp.bfloat16))
    send_grad = (weight_slot[:, None] * out_grad[token_of_slot].astype(jnp.float32)).astype(
        jnp.bfloat16
    )
    block_shape = (peer_count, local_count * capacity * 2 * model_width // 128, 128)
    send_both = jnp.concatenate([send_rows, send_grad], axis=1).reshape(block_shape)
    gate_width = gate_up_weight.shape[2]
    joined = jnp.concatenate([gate_up_weight[0], down_weight[0]], axis=1)
    recv_both, gathered = exchange(send_both, joined, True, 0)
    recv_both = recv_both.reshape(-1, 2 * model_width)
    expert_rows = recv_both[:, :model_width]
    grad_rows = recv_both[:, model_width:]
    full_joined = gathered.reshape(-1, joined.shape[1])
    full_gate_up = full_joined[:, :gate_width]
    full_down = full_joined[:, gate_width:]
    hidden, gate_part, up_part, sigmoid_gate, silu_gate = swiglu_forward(expert_rows, full_gate_up)
    produced = lax.dot_general(
        hidden, full_down, (((1,), (1,)), ((), ())), preferred_element_type=jnp.float32
    )
    down_parts = weight_blocks(grad_rows, hidden)
    hidden_grad = jnp.dot(grad_rows, full_down, preferred_element_type=jnp.float32)
    pre_grad = jnp.concatenate(
        [
            hidden_grad * up_part * sigmoid_gate * (1.0 + gate_part * (1.0 - sigmoid_gate)),
            hidden_grad * silu_gate,
        ],
        axis=1,
    ).astype(jnp.bfloat16)
    input_grad = lax.dot_general(
        pre_grad, full_gate_up, (((1,), (1,)), ((), ())), preferred_element_type=jnp.float32
    )
    back_both = jnp.concatenate(
        [produced.astype(jnp.bfloat16), input_grad.astype(jnp.bfloat16)], axis=1
    ).reshape(block_shape)
    returned, down_recv = exchange(back_both, down_parts, False, 1)
    returned = returned.reshape(slot_count, 2 * model_width)
    out_pairs = returned[:, :model_width][slot_of_pair]
    grad_pairs = returned[:, model_width:][slot_of_pair]
    weighted = probs_flat[:, None] * out_pairs.astype(jnp.float32)
    mixed = jnp.sum(weighted.reshape(tok_rows, top_count, model_width), axis=1).astype(jnp.bfloat16)
    token_grad = jnp.sum(
        grad_pairs.astype(jnp.float32).reshape(tok_rows, top_count, model_width), axis=1
    ).astype(jnp.bfloat16)
    down_grad = jnp.sum(down_recv.astype(jnp.float32), axis=0)[None].astype(jnp.bfloat16)
    return (mixed, token_grad, down_grad)


def solution(mesh):
    in_specs = (
        P(("dp", "expert"), None),
        P(("dp", "expert"), None),
        P(("dp", "expert"), None),
        P(("dp", "expert"), None),
        P("expert", "dp", None),
        P("expert", "dp", None),
    )
    out_specs = (P(("dp", "expert"), None), P(("dp", "expert"), None), P("expert", "dp", None))
    return jax.shard_map(shards, mesh=mesh, in_specs=in_specs, out_specs=out_specs, check_vma=False)
```

```python
import functools

import jax
import jax.numpy as jnp
from jax import lax
from jax.experimental import pallas as pl
from jax.experimental.pallas import tpu as pltpu
from jax.sharding import PartitionSpec as P

MESH = pl.DeviceIdType.MESH

loss_scale = 0.03125


def exchange_kernel(n_dp, n_ex, n_lo, bcast, ex_send, dp_send, ex_recv, dp_recv, send_sems, recv_sems, own_sems):
    q = lax.axis_index("dp")
    p = lax.axis_index("expert")
    n_hi = n_dp // n_lo
    row = q // n_lo
    lo = q % n_lo
    barrier = pltpu.get_barrier_semaphore()
    far = n_lo == 4 and n_ex % 8 == 0

    def peer_q(j):
        if not far:
            return q
        gap = lax.rem(j // 2 - p // 2 + 8 * n_ex, 4)
        return q + (gap // 2) * (1 - gap % 2) * (3 - 2 * lo)

    def greet_ex(k, c):
        j = lax.rem(p + k, n_ex)
        pl.semaphore_signal(barrier, 1, device_id=(peer_q(j), j), device_id_type=MESH)
        return c

    def greet_dp(k, c):
        pl.semaphore_signal(barrier, 1, device_id=(lax.rem(q + k, n_dp), p), device_id_type=MESH)
        return c

    lax.fori_loop(1, n_ex, greet_ex, 0)
    lax.fori_loop(1, n_dp, greet_dp, 0)
    pl.semaphore_wait(barrier, n_ex + n_dp - 2)

    def ex_copy(j, slot):
        return pltpu.make_async_remote_copy(
            src_ref=ex_send.at[j], dst_ref=ex_recv.at[slot], send_sem=send_sems.at[j],
            recv_sem=recv_sems.at[slot], device_id=(peer_q(j), j), device_id_type=MESH)

    def dp_copy(i, slot):
        src = dp_send if bcast else dp_send.at[i]
        return pltpu.make_async_remote_copy(
            src_ref=src, dst_ref=dp_recv.at[slot], send_sem=send_sems.at[n_ex + i],
            recv_sem=recv_sems.at[n_ex + slot], device_id=(i, p), device_id_type=MESH)

    def row_copy(r, slot_row, k):
        rows = pl.ds(pl.multiple_of(slot_row * n_lo, n_lo), n_lo)
        return pltpu.make_async_remote_copy(
            src_ref=dp_recv.at[rows], dst_ref=dp_recv.at[rows],
            send_sem=send_sems.at[n_ex + n_dp + k], recv_sem=recv_sems.at[n_ex + n_dp + slot_row],
            device_id=(r * n_lo + lo, p), device_id_type=MESH)

    def send_ex(k, c):
        ex_copy(lax.rem(p + k, n_ex), p).start()
        return c

    def send_dp(k, c):
        dp_copy(lax.rem(q + k, n_dp), q).start()
        return c

    def send_lo(k, c):
        dp_copy(row * n_lo + lax.rem(lo + k, n_lo), q).start()
        return c

    own_dp = pltpu.make_async_copy(dp_send if bcast else dp_send.at[q], dp_recv.at[q], own_sems.at[1])
    if bcast:
        lax.fori_loop(1, n_lo, send_lo, 0)
    else:
        lax.fori_loop(1, n_dp, send_dp, 0)
    own_dp.start()
    own_ex = pltpu.make_async_copy(ex_send.at[p], ex_recv.at[p], own_sems.at[0])
    own_ex.start()
    late = bcast and n_hi == 4
    if not late:
        lax.fori_loop(1, n_ex, send_ex, 0)

    def wait_ex(k, c):
        j = lax.rem(p + k, n_ex)
        ex_copy(j, p).wait_send()
        ex_copy(j, j).wait_recv()
        return c

    def wait_dp(k, c):
        i = lax.rem(q + k, n_dp)
        dp_copy(i, q).wait_send()
        dp_copy(i, i).wait_recv()
        return c

    def wait_lo(k, c):
        i = row * n_lo + lax.rem(lo + k, n_lo)
        dp_copy(i, q).wait_send()
        dp_copy(i, i).wait_recv()
        return c

    def send_hi(k, c):
        row_copy(lax.rem(row + k, n_hi), row, k).start()
        return c

    def wait_hi(k, c):
        r = lax.rem(row + k, n_hi)
        row_copy(r, row, k).wait_send()
        row_copy(r, r, k).wait_recv()
        return c

    def fwd_copy(start, count, target_row, s_idx, r_idx):
        rows = dp_recv.at[pl.ds(start, count)]
        return pltpu.make_async_remote_copy(
            src_ref=rows, dst_ref=rows, send_sem=send_sems.at[n_ex + n_dp + s_idx],
            recv_sem=recv_sems.at[n_ex + n_dp + r_idx],
            device_id=(target_row * n_lo + lo, p), device_id_type=MESH)

    if bcast and n_hi == 4:
        half = n_lo // 2
        up = lax.rem(row + 1, 4)
        dn = lax.rem(row + 3, 4)
        far_row = lax.rem(row + 2, 4)
        lax.fori_loop(1, n_lo, wait_lo, 0)
        own_dp.wait()
        to_up = fwd_copy(row * n_lo, n_lo, up, 0, row)
        to_dn = fwd_copy(row * n_lo, n_lo, dn, 1, row)
        to_up.start()
        to_dn.start()
        lax.fori_loop(1, n_ex, send_ex, 0)
        fwd_copy(dn * n_lo, n_lo, dn, 0, dn).wait_recv()
        fwd_copy(up * n_lo, n_lo, up, 1, up).wait_recv()
        pass_up = fwd_copy(dn * n_lo, half, up, 2, 4)
        pass_dn = fwd_copy(up * n_lo + half, n_lo - half, dn, 3, 5)
        pass_up.start()
        pass_dn.start()
        lax.fori_loop(1, n_ex, wait_ex, 0)
        fwd_copy(far_row * n_lo, half, up, 2, 4).wait_recv()
        fwd_copy(far_row * n_lo + half, n_lo - half, dn, 3, 5).wait_recv()
        to_up.wait_send()
        to_dn.wait_send()
        pass_up.wait_send()
        pass_dn.wait_send()
    elif bcast:
        lax.fori_loop(1, n_lo, wait_lo, 0)
        own_dp.wait()
        lax.fori_loop(1, n_hi, send_hi, 0)
        lax.fori_loop(1, n_ex, wait_ex, 0)
        lax.fori_loop(1, n_hi, wait_hi, 0)
    else:
        lax.fori_loop(1, n_ex, wait_ex, 0)
        lax.fori_loop(1, n_dp, wait_dp, 0)
        own_dp.wait()
    own_ex.wait()


def exchange(ex_send, dp_send, bcast, cid):
    n_dp = lax.axis_size("dp")
    n_ex = lax.axis_size("expert")
    dp_block = dp_send.shape if bcast else dp_send.shape[1:]
    n_lo = 4 if n_dp % 4 == 0 else n_dp
    return pl.pallas_call(
        functools.partial(exchange_kernel, n_dp, n_ex, n_lo, bcast),
        out_shape=(
            jax.ShapeDtypeStruct(ex_send.shape, ex_send.dtype),
            jax.ShapeDtypeStruct((n_dp,) + tuple(dp_block), dp_send.dtype),
        ),
        in_specs=[pl.BlockSpec(memory_space=pl.ANY)] * 2,
        out_specs=(pl.BlockSpec(memory_space=pl.ANY), pl.BlockSpec(memory_space=pl.ANY)),
        scratch_shapes=[
            pltpu.SemaphoreType.DMA((n_ex + n_dp + n_dp,)),
            pltpu.SemaphoreType.DMA((n_ex + n_dp + n_dp,)),
            pltpu.SemaphoreType.DMA((2,)),
        ],
        compiler_params=pltpu.CompilerParams(collective_id=cid, has_side_effects=True),
    )(ex_send, dp_send)


def swiglu_forward(expert_rows, gate_up_full):
    projected = jnp.dot(expert_rows, gate_up_full, preferred_element_type=jnp.float32)
    units = gate_up_full.shape[1] // 2
    gate_part = projected[:, :units]
    up_part = projected[:, units:]
    sigmoid_gate = jax.nn.sigmoid(gate_part)
    silu_gate = gate_part * sigmoid_gate
    hidden = (silu_gate * up_part).astype(jnp.bfloat16)
    return (hidden, gate_part, up_part, sigmoid_gate, silu_gate)


def weight_blocks(grad_rows, hidden):
    product = lax.dot_general(
        grad_rows, hidden, (((0,), (0,)), ((), ())), preferred_element_type=jnp.float32
    )
    parts = lax.axis_size("dp")
    blocks = (product * loss_scale).astype(jnp.bfloat16)
    return blocks.reshape(parts, blocks.shape[0] // parts, blocks.shape[1])


def shards(tokens, out_grad, routing, gate_probs, gate_up_weight, down_weight):
    peer_count = lax.axis_size("expert")
    local_count = gate_up_weight.shape[0]
    expert_count = peer_count * local_count
    tok_rows = tokens.shape[0]
    top_count = routing.shape[1]
    model_width = tokens.shape[1]
    capacity = max(2, 9 * tok_rows * top_count // (8 * expert_count))
    pair_count = tok_rows * top_count
    slot_count = expert_count * capacity
    flat_ids = routing.reshape(pair_count)
    onehot = (flat_ids[:, None] == jnp.arange(expert_count, dtype=jnp.int32)[None, :]).astype(
        jnp.int32
    )
    slot_rank = jnp.sum((jnp.cumsum(onehot, 0) - onehot) * onehot, 1)
    slot_of_pair = flat_ids * capacity + slot_rank
    pair_index = jnp.arange(pair_count, dtype=jnp.int32)
    matches = slot_of_pair[None, :] == jnp.arange(slot_count, dtype=jnp.int32)[:, None]
    filled = jnp.any(matches, axis=1)
    source = jnp.sum(jnp.where(matches, pair_index[None, :], 0), axis=1)
    token_of_slot = source // top_count
    probs_flat = gate_probs.reshape(pair_count)
    weight_slot = jnp.where(filled, probs_flat[source], jnp.float32(0.0))
    send_rows = jnp.where(filled[:, None], tokens[token_of_slot], jnp.zeros((), jnp.bfloat16))
    send_grad = (weight_slot[:, None] * out_grad[token_of_slot].astype(jnp.float32)).astype(
        jnp.bfloat16
    )
    block_shape = (peer_count, local_count * capacity * 2 * model_width // 128, 128)
    send_both = jnp.concatenate([send_rows, send_grad], axis=1).reshape(block_shape)
    gate_width = gate_up_weight.shape[2]
    joined = jnp.concatenate([gate_up_weight[0], down_weight[0]], axis=1)
    recv_both, gathered = exchange(send_both, joined, True, 0)
    recv_both = recv_both.reshape(-1, 2 * model_width)
    expert_rows = recv_both[:, :model_width]
    grad_rows = recv_both[:, model_width:]
    full_joined = gathered.reshape(-1, joined.shape[1])
    full_gate_up = full_joined[:, :gate_width]
    full_down = full_joined[:, gate_width:]
    hidden, gate_part, up_part, sigmoid_gate, silu_gate = swiglu_forward(expert_rows, full_gate_up)
    produced = lax.dot_general(
        hidden, full_down, (((1,), (1,)), ((), ())), preferred_element_type=jnp.float32
    )
    down_parts = weight_blocks(grad_rows, hidden)
    hidden_grad = jnp.dot(grad_rows, full_down, preferred_element_type=jnp.float32)
    pre_grad = jnp.concatenate(
        [
            hidden_grad * up_part * sigmoid_gate * (1.0 + gate_part * (1.0 - sigmoid_gate)),
            hidden_grad * silu_gate,
        ],
        axis=1,
    ).astype(jnp.bfloat16)
    input_grad = lax.dot_general(
        pre_grad, full_gate_up, (((1,), (1,)), ((), ())), preferred_element_type=jnp.float32
    )
    back_both = jnp.concatenate(
        [produced.astype(jnp.bfloat16), input_grad.astype(jnp.bfloat16)], axis=1
    ).reshape(block_shape)
    returned, down_recv = exchange(back_both, down_parts, False, 1)
    returned = returned.reshape(slot_count, 2 * model_width)
    out_pairs = returned[:, :model_width][slot_of_pair]
    grad_pairs = returned[:, model_width:][slot_of_pair]
    weighted = probs_flat[:, None] * out_pairs.astype(jnp.float32)
    mixed = jnp.sum(weighted.reshape(tok_rows, top_count, model_width), axis=1).astype(jnp.bfloat16)
    token_grad = jnp.sum(
        grad_pairs.astype(jnp.float32).reshape(tok_rows, top_count, model_width), axis=1
    ).astype(jnp.bfloat16)
    down_grad = jnp.sum(down_recv.astype(jnp.float32), axis=0)[None].astype(jnp.bfloat16)
    return (mixed, token_grad, down_grad)


def solution(mesh):
    in_specs = (
        P(("dp", "expert"), None),
        P(("dp", "expert"), None),
        P(("dp", "expert"), None),
        P(("dp", "expert"), None),
        P("expert", "dp", None),
        P("expert", "dp", None),
    )
    out_specs = (P(("dp", "expert"), None), P(("dp", "expert"), None), P("expert", "dp", None))
    return jax.shard_map(shards, mesh=mesh, in_specs=in_specs, out_specs=out_specs, check_vma=False)
```

```python
import functools

import jax
import jax.numpy as jnp
from jax import lax
from jax.experimental import pallas as pl
from jax.experimental.pallas import tpu as pltpu
from jax.sharding import PartitionSpec as P

MESH = pl.DeviceIdType.MESH

loss_scale = 0.03125


def exchange_kernel(n_dp, n_ex, n_lo, bcast, ex_send, dp_send, ex_recv, dp_recv, send_sems, recv_sems, own_sems):
    q = lax.axis_index("dp")
    p = lax.axis_index("expert")
    n_hi = n_dp // n_lo
    row = q // n_lo
    lo = q % n_lo
    barrier = pltpu.get_barrier_semaphore()
    far = n_lo == 4 and n_ex % 8 == 0

    def peer_q(j):
        if not far:
            return q
        gap = lax.rem(j // 2 - p // 2 + 8 * n_ex, 4)
        return q + (gap // 2) * (1 - gap % 2) * (3 - 2 * lo)

    def greet_ex(k, c):
        j = lax.rem(p + k, n_ex)
        pl.semaphore_signal(barrier, 1, device_id=(peer_q(j), j), device_id_type=MESH)
        return c

    def greet_dp(k, c):
        pl.semaphore_signal(barrier, 1, device_id=(lax.rem(q + k, n_dp), p), device_id_type=MESH)
        return c

    lax.fori_loop(1, n_ex, greet_ex, 0)
    lax.fori_loop(1, n_dp, greet_dp, 0)
    pl.semaphore_wait(barrier, n_ex + n_dp - 2)

    def ex_copy(j, slot):
        return pltpu.make_async_remote_copy(
            src_ref=ex_send.at[j], dst_ref=ex_recv.at[slot], send_sem=send_sems.at[j],
            recv_sem=recv_sems.at[slot], device_id=(peer_q(j), j), device_id_type=MESH)

    def dp_copy(i, slot):
        src = dp_send if bcast else dp_send.at[i]
        return pltpu.make_async_remote_copy(
            src_ref=src, dst_ref=dp_recv.at[slot], send_sem=send_sems.at[n_ex + i],
            recv_sem=recv_sems.at[n_ex + slot], device_id=(i, p), device_id_type=MESH)

    def row_copy(r, slot_row, k):
        rows = pl.ds(pl.multiple_of(slot_row * n_lo, n_lo), n_lo)
        return pltpu.make_async_remote_copy(
            src_ref=dp_recv.at[rows], dst_ref=dp_recv.at[rows],
            send_sem=send_sems.at[n_ex + n_dp + k], recv_sem=recv_sems.at[n_ex + n_dp + slot_row],
            device_id=(r * n_lo + lo, p), device_id_type=MESH)

    def send_ex(k, c):
        ex_copy(lax.rem(p + k, n_ex), p).start()
        return c

    def send_dp(k, c):
        dp_copy(lax.rem(q + k, n_dp), q).start()
        return c

    def send_lo(k, c):
        dp_copy(row * n_lo + lax.rem(lo + k, n_lo), q).start()
        return c

    own_dp = pltpu.make_async_copy(dp_send if bcast else dp_send.at[q], dp_recv.at[q], own_sems.at[1])
    if bcast:
        lax.fori_loop(1, n_lo, send_lo, 0)
    else:
        lax.fori_loop(1, n_dp, send_dp, 0)
    own_dp.start()
    own_ex = pltpu.make_async_copy(ex_send.at[p], ex_recv.at[p], own_sems.at[0])
    own_ex.start()
    late = bcast and n_hi == 4
    if not late:
        lax.fori_loop(1, n_ex, send_ex, 0)

    def wait_ex(k, c):
        j = lax.rem(p + k, n_ex)
        ex_copy(j, p).wait_send()
        ex_copy(j, j).wait_recv()
        return c

    def wait_dp(k, c):
        i = lax.rem(q + k, n_dp)
        dp_copy(i, q).wait_send()
        dp_copy(i, i).wait_recv()
        return c

    def wait_lo(k, c):
        i = row * n_lo + lax.rem(lo + k, n_lo)
        dp_copy(i, q).wait_send()
        dp_copy(i, i).wait_recv()
        return c

    def send_hi(k, c):
        row_copy(lax.rem(row + k, n_hi), row, k).start()
        return c

    def wait_hi(k, c):
        r = lax.rem(row + k, n_hi)
        row_copy(r, row, k).wait_send()
        row_copy(r, r, k).wait_recv()
        return c

    def fwd_copy(start, count, target_row, s_idx, r_idx):
        rows = dp_recv.at[pl.ds(start, count)]
        return pltpu.make_async_remote_copy(
            src_ref=rows, dst_ref=rows, send_sem=send_sems.at[n_ex + n_dp + s_idx],
            recv_sem=recv_sems.at[n_ex + n_dp + r_idx],
            device_id=(target_row * n_lo + lo, p), device_id_type=MESH)

    if bcast and n_hi == 4:
        half = n_lo // 2
        up = lax.rem(row + 1, 4)
        dn = lax.rem(row + 3, 4)
        far_row = lax.rem(row + 2, 4)
        lax.fori_loop(1, n_lo, wait_lo, 0)
        own_dp.wait()
        to_up = fwd_copy(row * n_lo, n_lo, up, 0, row)
        to_dn = fwd_copy(row * n_lo, n_lo, dn, 1, row)
        to_up.start()
        to_dn.start()
        lax.fori_loop(1, n_ex, send_ex, 0)
        fwd_copy(dn * n_lo, n_lo, dn, 0, dn).wait_recv()
        fwd_copy(up * n_lo, n_lo, up, 1, up).wait_recv()
        pass_up = fwd_copy(dn * n_lo, half, up, 2, 4)
        pass_dn = fwd_copy(up * n_lo + half, n_lo - half, dn, 3, 5)
        pass_up.start()
        pass_dn.start()
        lax.fori_loop(1, n_ex, wait_ex, 0)
        fwd_copy(far_row * n_lo, half, up, 2, 4).wait_recv()
        fwd_copy(far_row * n_lo + half, n_lo - half, dn, 3, 5).wait_recv()
        to_up.wait_send()
        to_dn.wait_send()
        pass_up.wait_send()
        pass_dn.wait_send()
    elif bcast:
        lax.fori_loop(1, n_lo, wait_lo, 0)
        own_dp.wait()
        lax.fori_loop(1, n_hi, send_hi, 0)
        lax.fori_loop(1, n_ex, wait_ex, 0)
        lax.fori_loop(1, n_hi, wait_hi, 0)
    else:
        lax.fori_loop(1, n_ex, wait_ex, 0)
        lax.fori_loop(1, n_dp, wait_dp, 0)
        own_dp.wait()
    own_ex.wait()


def exchange(ex_send, dp_send, bcast, cid):
    n_dp = lax.axis_size("dp")
    n_ex = lax.axis_size("expert")
    dp_block = dp_send.shape if bcast else dp_send.shape[1:]
    n_lo = 4 if n_dp % 4 == 0 else n_dp
    return pl.pallas_call(
        functools.partial(exchange_kernel, n_dp, n_ex, n_lo, bcast),
        out_shape=(
            jax.ShapeDtypeStruct(ex_send.shape, ex_send.dtype),
            jax.ShapeDtypeStruct((n_dp,) + tuple(dp_block), dp_send.dtype),
        ),
        in_specs=[pl.BlockSpec(memory_space=pl.ANY)] * 2,
        out_specs=(pl.BlockSpec(memory_space=pl.ANY), pl.BlockSpec(memory_space=pl.ANY)),
        scratch_shapes=[
            pltpu.SemaphoreType.DMA((n_ex + n_dp + n_dp,)),
            pltpu.SemaphoreType.DMA((n_ex + n_dp + n_dp,)),
            pltpu.SemaphoreType.DMA((2,)),
        ],
        compiler_params=pltpu.CompilerParams(collective_id=cid, has_side_effects=True),
    )(ex_send, dp_send)


def swiglu_forward(expert_rows, gate_up_full):
    projected = jnp.dot(expert_rows, gate_up_full, preferred_element_type=jnp.float32)
    units = gate_up_full.shape[1] // 2
    gate_part = projected[:, :units]
    up_part = projected[:, units:]
    sigmoid_gate = jax.nn.sigmoid(gate_part)
    silu_gate = gate_part * sigmoid_gate
    hidden = (silu_gate * up_part).astype(jnp.bfloat16)
    return (hidden, gate_part, up_part, sigmoid_gate, silu_gate)


def weight_blocks(grad_rows, hidden):
    product = lax.dot_general(
        grad_rows, hidden, (((0,), (0,)), ((), ())), preferred_element_type=jnp.float32
    )
    parts = lax.axis_size("dp")
    blocks = (product * loss_scale).astype(jnp.bfloat16)
    return blocks.reshape(parts, blocks.shape[0] // parts, blocks.shape[1])


def shards(tokens, out_grad, routing, gate_probs, gate_up_weight, down_weight):
    peer_count = lax.axis_size("expert")
    local_count = gate_up_weight.shape[0]
    expert_count = peer_count * local_count
    tok_rows = tokens.shape[0]
    top_count = routing.shape[1]
    model_width = tokens.shape[1]
    capacity = max(2, 9 * tok_rows * top_count // (8 * expert_count))
    pair_count = tok_rows * top_count
    slot_count = expert_count * capacity
    flat_ids = routing.reshape(pair_count)
    onehot = (flat_ids[:, None] == jnp.arange(expert_count, dtype=jnp.int32)[None, :]).astype(
        jnp.int32
    )
    slot_rank = jnp.sum((jnp.cumsum(onehot, 0) - onehot) * onehot, 1)
    slot_of_pair = flat_ids * capacity + slot_rank
    pair_index = jnp.arange(pair_count, dtype=jnp.int32)
    matches = slot_of_pair[None, :] == jnp.arange(slot_count, dtype=jnp.int32)[:, None]
    filled = jnp.any(matches, axis=1)
    source = jnp.sum(jnp.where(matches, pair_index[None, :], 0), axis=1)
    token_of_slot = source // top_count
    probs_flat = gate_probs.reshape(pair_count)
    weight_slot = jnp.where(filled, probs_flat[source], jnp.float32(0.0))
    send_rows = jnp.where(filled[:, None], tokens[token_of_slot], jnp.zeros((), jnp.bfloat16))
    send_grad = (weight_slot[:, None] * out_grad[token_of_slot].astype(jnp.float32)).astype(
        jnp.bfloat16
    )
    block_shape = (peer_count, local_count * capacity * 2 * model_width // 128, 128)
    send_both = jnp.concatenate([send_rows, send_grad], axis=1).reshape(block_shape)
    gate_width = gate_up_weight.shape[2]
    joined = jnp.concatenate([gate_up_weight[0], down_weight[0]], axis=1)
    recv_both, gathered = exchange(send_both, joined, True, 0)
    recv_both = recv_both.reshape(-1, 2 * model_width)
    expert_rows = recv_both[:, :model_width]
    grad_rows = recv_both[:, model_width:]
    full_joined = gathered.reshape(-1, joined.shape[1])
    full_gate_up = full_joined[:, :gate_width]
    full_down = full_joined[:, gate_width:]
    hidden, gate_part, up_part, sigmoid_gate, silu_gate = swiglu_forward(expert_rows, full_gate_up)
    produced = lax.dot_general(
        hidden, full_down, (((1,), (1,)), ((), ())), preferred_element_type=jnp.float32
    )
    down_parts = weight_blocks(grad_rows, hidden)
    hidden_grad = jnp.dot(grad_rows, full_down, preferred_element_type=jnp.float32)
    pre_grad = jnp.concatenate(
        [
            hidden_grad * up_part * sigmoid_gate * (1.0 + gate_part * (1.0 - sigmoid_gate)),
            hidden_grad * silu_gate,
        ],
        axis=1,
    ).astype(jnp.bfloat16)
    input_grad = lax.dot_general(
        pre_grad, full_gate_up, (((1,), (1,)), ((), ())), preferred_element_type=jnp.float32
    )
    back_both = jnp.concatenate(
        [produced.astype(jnp.bfloat16), input_grad.astype(jnp.bfloat16)], axis=1
    ).reshape(block_shape)
    returned, down_recv = exchange(back_both, down_parts, False, 1)
    chunks = model_width // 128
    pairs = returned.reshape(slot_count, 2 * chunks, 128)[slot_of_pair]
    out_pairs = pairs[:, :chunks]
    grad_pairs = pairs[:, chunks:]
    weighted = probs_flat[:, None, None] * out_pairs.astype(jnp.float32)
    mixed = jnp.sum(weighted.reshape(tok_rows, top_count, model_width), axis=1).astype(jnp.bfloat16)
    token_grad = jnp.sum(
        grad_pairs.astype(jnp.float32).reshape(tok_rows, top_count, model_width), axis=1
    ).astype(jnp.bfloat16)
    down_grad = jnp.sum(down_recv.astype(jnp.float32), axis=0)[None].astype(jnp.bfloat16)
    return (mixed, token_grad, down_grad)


def solution(mesh):
    in_specs = (
        P(("dp", "expert"), None),
        P(("dp", "expert"), None),
        P(("dp", "expert"), None),
        P(("dp", "expert"), None),
        P("expert", "dp", None),
        P("expert", "dp", None),
    )
    out_specs = (P(("dp", "expert"), None), P(("dp", "expert"), None), P("expert", "dp", None))
    return jax.shard_map(shards, mesh=mesh, in_specs=in_specs, out_specs=out_specs, check_vma=False)
```

```python
import functools

import jax
import jax.numpy as jnp
from jax import lax
from jax.experimental import pallas as pl
from jax.experimental.pallas import tpu as pltpu
from jax.sharding import PartitionSpec as P

MESH = pl.DeviceIdType.MESH

loss_scale = 0.03125


def exchange_kernel(n_dp, n_ex, n_lo, bcast, ex_send, dp_send, ex_recv, dp_recv, send_sems, recv_sems, own_sems):
    q = lax.axis_index("dp")
    p = lax.axis_index("expert")
    n_hi = n_dp // n_lo
    row = q // n_lo
    lo = q % n_lo
    barrier = pltpu.get_barrier_semaphore()
    far = n_lo == 4 and n_ex % 8 == 0

    def peer_q(j):
        if not far:
            return q
        gap = lax.rem(j // 2 - p // 2 + 8 * n_ex, 4)
        return q + (gap // 2) * (1 - gap % 2) * (3 - 2 * lo)

    def greet_ex(k, c):
        j = lax.rem(p + k, n_ex)
        pl.semaphore_signal(barrier, 1, device_id=(peer_q(j), j), device_id_type=MESH)
        return c

    def greet_dp(k, c):
        pl.semaphore_signal(barrier, 1, device_id=(lax.rem(q + k, n_dp), p), device_id_type=MESH)
        return c

    lax.fori_loop(1, n_ex, greet_ex, 0)
    lax.fori_loop(1, n_dp, greet_dp, 0)
    pl.semaphore_wait(barrier, n_ex + n_dp - 2)

    def ex_copy(j, slot):
        return pltpu.make_async_remote_copy(
            src_ref=ex_send.at[j], dst_ref=ex_recv.at[slot], send_sem=send_sems.at[j],
            recv_sem=recv_sems.at[slot], device_id=(peer_q(j), j), device_id_type=MESH)

    def dp_copy(i, slot):
        src = dp_send if bcast else dp_send.at[i]
        return pltpu.make_async_remote_copy(
            src_ref=src, dst_ref=dp_recv.at[slot], send_sem=send_sems.at[n_ex + i],
            recv_sem=recv_sems.at[n_ex + slot], device_id=(i, p), device_id_type=MESH)

    def row_copy(r, slot_row, k):
        rows = pl.ds(pl.multiple_of(slot_row * n_lo, n_lo), n_lo)
        return pltpu.make_async_remote_copy(
            src_ref=dp_recv.at[rows], dst_ref=dp_recv.at[rows],
            send_sem=send_sems.at[n_ex + n_dp + k], recv_sem=recv_sems.at[n_ex + n_dp + slot_row],
            device_id=(r * n_lo + lo, p), device_id_type=MESH)

    def send_ex(k, c):
        ex_copy(lax.rem(p + k, n_ex), p).start()
        return c

    def send_dp(k, c):
        dp_copy(lax.rem(q + k, n_dp), q).start()
        return c

    def send_lo(k, c):
        dp_copy(row * n_lo + lax.rem(lo + k, n_lo), q).start()
        return c

    own_dp = pltpu.make_async_copy(dp_send if bcast else dp_send.at[q], dp_recv.at[q], own_sems.at[1])
    if bcast:
        lax.fori_loop(1, n_lo, send_lo, 0)
    else:
        lax.fori_loop(1, n_dp, send_dp, 0)
    own_dp.start()
    own_ex = pltpu.make_async_copy(ex_send.at[p], ex_recv.at[p], own_sems.at[0])
    own_ex.start()
    late = bcast and n_hi == 4
    n_x = n_ex // 8

    def near_j(m):
        a = m // 2
        return lax.rem(p // 8 + a, n_x) * 8 + lax.rem(p // 2, 4) * 2 + lax.rem(p + m, 2)

    def far_j(m):
        b = 1 + m // (2 * n_x)
        a = (m // 2) % n_x
        return lax.rem(p // 8 + a, n_x) * 8 + lax.rem(p // 2 + b, 4) * 2 + lax.rem(p + m, 2)

    def send_near(m, c):
        ex_copy(near_j(m), p).start()
        return c

    def send_far(m, c):
        ex_copy(far_j(m), p).start()
        return c

    split = late and far
    if split:
        lax.fori_loop(1, 2 * n_x, send_near, 0)
    elif not late:
        lax.fori_loop(1, n_ex, send_ex, 0)

    def wait_ex(k, c):
        j = lax.rem(p + k, n_ex)
        ex_copy(j, p).wait_send()
        ex_copy(j, j).wait_recv()
        return c

    def wait_dp(k, c):
        i = lax.rem(q + k, n_dp)
        dp_copy(i, q).wait_send()
        dp_copy(i, i).wait_recv()
        return c

    def wait_lo(k, c):
        i = row * n_lo + lax.rem(lo + k, n_lo)
        dp_copy(i, q).wait_send()
        dp_copy(i, i).wait_recv()
        return c

    def send_hi(k, c):
        row_copy(lax.rem(row + k, n_hi), row, k).start()
        return c

    def wait_hi(k, c):
        r = lax.rem(row + k, n_hi)
        row_copy(r, row, k).wait_send()
        row_copy(r, r, k).wait_recv()
        return c

    def fwd_copy(start, count, target_row, s_idx, r_idx):
        rows = dp_recv.at[pl.ds(start, count)]
        return pltpu.make_async_remote_copy(
            src_ref=rows, dst_ref=rows, send_sem=send_sems.at[n_ex + n_dp + s_idx],
            recv_sem=recv_sems.at[n_ex + n_dp + r_idx],
            device_id=(target_row * n_lo + lo, p), device_id_type=MESH)

    if bcast and n_hi == 4:
        half = n_lo // 2
        up = lax.rem(row + 1, 4)
        dn = lax.rem(row + 3, 4)
        far_row = lax.rem(row + 2, 4)
        lax.fori_loop(1, n_lo, wait_lo, 0)
        own_dp.wait()
        to_up = fwd_copy(row * n_lo, n_lo, up, 0, row)
        to_dn = fwd_copy(row * n_lo, n_lo, dn, 1, row)
        to_up.start()
        to_dn.start()
        if split:
            lax.fori_loop(0, 6 * n_x, send_far, 0)
        else:
            lax.fori_loop(1, n_ex, send_ex, 0)
        fwd_copy(dn * n_lo, n_lo, dn, 0, dn).wait_recv()
        fwd_copy(up * n_lo, n_lo, up, 1, up).wait_recv()
        pass_up = fwd_copy(dn * n_lo, half, up, 2, 4)
        pass_dn = fwd_copy(up * n_lo + half, n_lo - half, dn, 3, 5)
        pass_up.start()
        pass_dn.start()
        lax.fori_loop(1, n_ex, wait_ex, 0)
        fwd_copy(far_row * n_lo, half, up, 2, 4).wait_recv()
        fwd_copy(far_row * n_lo + half, n_lo - half, dn, 3, 5).wait_recv()
        to_up.wait_send()
        to_dn.wait_send()
        pass_up.wait_send()
        pass_dn.wait_send()
    elif bcast:
        lax.fori_loop(1, n_lo, wait_lo, 0)
        own_dp.wait()
        lax.fori_loop(1, n_hi, send_hi, 0)
        lax.fori_loop(1, n_ex, wait_ex, 0)
        lax.fori_loop(1, n_hi, wait_hi, 0)
    else:
        lax.fori_loop(1, n_ex, wait_ex, 0)
        lax.fori_loop(1, n_dp, wait_dp, 0)
        own_dp.wait()
    own_ex.wait()


def exchange(ex_send, dp_send, bcast, cid):
    n_dp = lax.axis_size("dp")
    n_ex = lax.axis_size("expert")
    dp_block = dp_send.shape if bcast else dp_send.shape[1:]
    n_lo = 4 if n_dp % 4 == 0 else n_dp
    return pl.pallas_call(
        functools.partial(exchange_kernel, n_dp, n_ex, n_lo, bcast),
        out_shape=(
            jax.ShapeDtypeStruct(ex_send.shape, ex_send.dtype),
            jax.ShapeDtypeStruct((n_dp,) + tuple(dp_block), dp_send.dtype),
        ),
        in_specs=[pl.BlockSpec(memory_space=pl.ANY)] * 2,
        out_specs=(pl.BlockSpec(memory_space=pl.ANY), pl.BlockSpec(memory_space=pl.ANY)),
        scratch_shapes=[
            pltpu.SemaphoreType.DMA((n_ex + n_dp + n_dp,)),
            pltpu.SemaphoreType.DMA((n_ex + n_dp + n_dp,)),
            pltpu.SemaphoreType.DMA((2,)),
        ],
        compiler_params=pltpu.CompilerParams(collective_id=cid, has_side_effects=True),
    )(ex_send, dp_send)


def swiglu_forward(expert_rows, gate_up_full):
    projected = jnp.dot(expert_rows, gate_up_full, preferred_element_type=jnp.float32)
    units = gate_up_full.shape[1] // 2
    gate_part = projected[:, :units]
    up_part = projected[:, units:]
    sigmoid_gate = jax.nn.sigmoid(gate_part)
    silu_gate = gate_part * sigmoid_gate
    hidden = (silu_gate * up_part).astype(jnp.bfloat16)
    return (hidden, gate_part, up_part, sigmoid_gate, silu_gate)


def weight_blocks(grad_rows, hidden):
    product = lax.dot_general(
        grad_rows, hidden, (((0,), (0,)), ((), ())), preferred_element_type=jnp.float32
    )
    parts = lax.axis_size("dp")
    blocks = (product * loss_scale).astype(jnp.bfloat16)
    return blocks.reshape(parts, blocks.shape[0] // parts, blocks.shape[1])


def shards(tokens, out_grad, routing, gate_probs, gate_up_weight, down_weight):
    peer_count = lax.axis_size("expert")
    local_count = gate_up_weight.shape[0]
    expert_count = peer_count * local_count
    tok_rows = tokens.shape[0]
    top_count = routing.shape[1]
    model_width = tokens.shape[1]
    capacity = max(2, 9 * tok_rows * top_count // (8 * expert_count))
    pair_count = tok_rows * top_count
    slot_count = expert_count * capacity
    flat_ids = routing.reshape(pair_count)
    onehot = (flat_ids[:, None] == jnp.arange(expert_count, dtype=jnp.int32)[None, :]).astype(
        jnp.int32
    )
    slot_rank = jnp.sum((jnp.cumsum(onehot, 0) - onehot) * onehot, 1)
    slot_of_pair = flat_ids * capacity + slot_rank
    pair_index = jnp.arange(pair_count, dtype=jnp.int32)
    matches = slot_of_pair[None, :] == jnp.arange(slot_count, dtype=jnp.int32)[:, None]
    filled = jnp.any(matches, axis=1)
    source = jnp.sum(jnp.where(matches, pair_index[None, :], 0), axis=1)
    token_of_slot = source // top_count
    probs_flat = gate_probs.reshape(pair_count)
    weight_slot = jnp.where(filled, probs_flat[source], jnp.float32(0.0))
    send_rows = jnp.where(filled[:, None], tokens[token_of_slot], jnp.zeros((), jnp.bfloat16))
    send_grad = (weight_slot[:, None] * out_grad[token_of_slot].astype(jnp.float32)).astype(
        jnp.bfloat16
    )
    block_shape = (peer_count, local_count * capacity * 2 * model_width // 128, 128)
    send_both = jnp.concatenate([send_rows, send_grad], axis=1).reshape(block_shape)
    gate_width = gate_up_weight.shape[2]
    joined = jnp.concatenate([gate_up_weight[0], down_weight[0]], axis=1)
    recv_both, gathered = exchange(send_both, joined, True, 0)
    recv_both = recv_both.reshape(-1, 2 * model_width)
    expert_rows = recv_both[:, :model_width]
    grad_rows = recv_both[:, model_width:]
    full_joined = gathered.reshape(-1, joined.shape[1])
    full_gate_up = full_joined[:, :gate_width]
    full_down = full_joined[:, gate_width:]
    hidden, gate_part, up_part, sigmoid_gate, silu_gate = swiglu_forward(expert_rows, full_gate_up)
    produced = lax.dot_general(
        hidden, full_down, (((1,), (1,)), ((), ())), preferred_element_type=jnp.float32
    )
    down_parts = weight_blocks(grad_rows, hidden)
    hidden_grad = jnp.dot(grad_rows, full_down, preferred_element_type=jnp.float32)
    pre_grad = jnp.concatenate(
        [
            hidden_grad * up_part * sigmoid_gate * (1.0 + gate_part * (1.0 - sigmoid_gate)),
            hidden_grad * silu_gate,
        ],
        axis=1,
    ).astype(jnp.bfloat16)
    input_grad = lax.dot_general(
        pre_grad, full_gate_up, (((1,), (1,)), ((), ())), preferred_element_type=jnp.float32
    )
    back_both = jnp.concatenate(
        [produced.astype(jnp.bfloat16), input_grad.astype(jnp.bfloat16)], axis=1
    ).reshape(block_shape)
    returned, down_recv = exchange(back_both, down_parts, False, 1)
    chunks = model_width // 128
    pairs = returned.reshape(slot_count, 2 * chunks, 128)[slot_of_pair]
    out_pairs = pairs[:, :chunks]
    grad_pairs = pairs[:, chunks:]
    weighted = probs_flat[:, None, None] * out_pairs.astype(jnp.float32)
    mixed = jnp.sum(weighted.reshape(tok_rows, top_count, model_width), axis=1).astype(jnp.bfloat16)
    token_grad = jnp.sum(
        grad_pairs.astype(jnp.float32).reshape(tok_rows, top_count, model_width), axis=1
    ).astype(jnp.bfloat16)
    down_grad = jnp.sum(down_recv.astype(jnp.float32), axis=0)[None].astype(jnp.bfloat16)
    return (mixed, token_grad, down_grad)


def solution(mesh):
    in_specs = (
        P(("dp", "expert"), None),
        P(("dp", "expert"), None),
        P(("dp", "expert"), None),
        P(("dp", "expert"), None),
        P("expert", "dp", None),
        P("expert", "dp", None),
    )
    out_specs = (P(("dp", "expert"), None), P(("dp", "expert"), None), P("expert", "dp", None))
    return jax.shard_map(shards, mesh=mesh, in_specs=in_specs, out_specs=out_specs, check_vma=False)
```

```python
import functools

import jax
import jax.numpy as jnp
from jax import lax
from jax.experimental import pallas as pl
from jax.experimental.pallas import tpu as pltpu
from jax.sharding import PartitionSpec as P

MESH = pl.DeviceIdType.MESH

loss_scale = 0.03125


def exchange_kernel(n_dp, n_ex, n_lo, bcast, ex_send, dp_send, ex_recv, dp_recv, send_sems, recv_sems, own_sems):
    q = lax.axis_index("dp")
    p = lax.axis_index("expert")
    n_hi = n_dp // n_lo
    row = q // n_lo
    lo = q % n_lo
    barrier = pltpu.get_barrier_semaphore()
    far = n_lo == 4 and n_ex % 8 == 0

    def peer_q(j):
        if not far:
            return q
        gap = lax.rem(j // 2 - p // 2 + 8 * n_ex, 4)
        return q + (gap // 2) * (1 - gap % 2) * (3 - 2 * lo)

    def greet_ex(k, c):
        j = lax.rem(p + k, n_ex)
        pl.semaphore_signal(barrier, 1, device_id=(peer_q(j), j), device_id_type=MESH)
        return c

    def greet_dp(k, c):
        pl.semaphore_signal(barrier, 1, device_id=(lax.rem(q + k, n_dp), p), device_id_type=MESH)
        return c

    lax.fori_loop(1, n_ex, greet_ex, 0)
    lax.fori_loop(1, n_dp, greet_dp, 0)
    pl.semaphore_wait(barrier, n_ex + n_dp - 2)

    def ex_copy(j, slot):
        return pltpu.make_async_remote_copy(
            src_ref=ex_send.at[j], dst_ref=ex_recv.at[slot], send_sem=send_sems.at[j],
            recv_sem=recv_sems.at[slot], device_id=(peer_q(j), j), device_id_type=MESH)

    def dp_copy(i, slot):
        src = dp_send if bcast else dp_send.at[i]
        return pltpu.make_async_remote_copy(
            src_ref=src, dst_ref=dp_recv.at[slot], send_sem=send_sems.at[n_ex + i],
            recv_sem=recv_sems.at[n_ex + slot], device_id=(i, p), device_id_type=MESH)

    def row_copy(r, slot_row, k):
        rows = pl.ds(pl.multiple_of(slot_row * n_lo, n_lo), n_lo)
        return pltpu.make_async_remote_copy(
            src_ref=dp_recv.at[rows], dst_ref=dp_recv.at[rows],
            send_sem=send_sems.at[n_ex + n_dp + k], recv_sem=recv_sems.at[n_ex + n_dp + slot_row],
            device_id=(r * n_lo + lo, p), device_id_type=MESH)

    def send_ex(k, c):
        ex_copy(lax.rem(p + k, n_ex), p).start()
        return c

    def send_dp(k, c):
        dp_copy(lax.rem(q + k, n_dp), q).start()
        return c

    def send_lo(k, c):
        dp_copy(row * n_lo + lax.rem(lo + k, n_lo), q).start()
        return c

    own_dp = pltpu.make_async_copy(dp_send if bcast else dp_send.at[q], dp_recv.at[q], own_sems.at[1])
    chain = bcast and n_hi == 4 and n_lo == 4

    def lo_copy(origin, target, s_idx, own):
        slot = row * n_lo + origin
        return pltpu.make_async_remote_copy(
            src_ref=dp_send if own else dp_recv.at[slot], dst_ref=dp_recv.at[slot],
            send_sem=send_sems.at[n_ex + s_idx], recv_sem=recv_sems.at[n_ex + slot],
            device_id=(row * n_lo + target, p), device_id_type=MESH)

    if chain:
        @pl.when(lo < n_lo - 1)
        def _():
            lo_copy(lo, lo + 1, 0, True).start()

        @pl.when(lo > 0)
        def _():
            lo_copy(lo, lo - 1, 4, True).start()
    elif bcast:
        lax.fori_loop(1, n_lo, send_lo, 0)
    else:
        lax.fori_loop(1, n_dp, send_dp, 0)
    own_dp.start()
    own_ex = pltpu.make_async_copy(ex_send.at[p], ex_recv.at[p], own_sems.at[0])
    own_ex.start()
    late = bcast and n_hi == 4
    n_x = n_ex // 8

    def near_j(m):
        a = m // 2
        return lax.rem(p // 8 + a, n_x) * 8 + lax.rem(p // 2, 4) * 2 + lax.rem(p + m, 2)

    def far_j(m):
        b = 1 + m // (2 * n_x)
        a = (m // 2) % n_x
        return lax.rem(p // 8 + a, n_x) * 8 + lax.rem(p // 2 + b, 4) * 2 + lax.rem(p + m, 2)

    def send_near(m, c):
        ex_copy(near_j(m), p).start()
        return c

    def send_far(m, c):
        ex_copy(far_j(m), p).start()
        return c

    split = late and far
    if split:
        lax.fori_loop(1, 2 * n_x, send_near, 0)
    elif not late:
        lax.fori_loop(1, n_ex, send_ex, 0)

    def wait_ex(k, c):
        j = lax.rem(p + k, n_ex)
        ex_copy(j, p).wait_send()
        ex_copy(j, j).wait_recv()
        return c

    def wait_dp(k, c):
        i = lax.rem(q + k, n_dp)
        dp_copy(i, q).wait_send()
        dp_copy(i, i).wait_recv()
        return c

    def wait_lo(k, c):
        i = row * n_lo + lax.rem(lo + k, n_lo)
        dp_copy(i, q).wait_send()
        dp_copy(i, i).wait_recv()
        return c

    def send_hi(k, c):
        row_copy(lax.rem(row + k, n_hi), row, k).start()
        return c

    def wait_hi(k, c):
        r = lax.rem(row + k, n_hi)
        row_copy(r, row, k).wait_send()
        row_copy(r, r, k).wait_recv()
        return c

    def fwd_copy(start, count, target_row, s_idx, r_idx):
        rows = dp_recv.at[pl.ds(start, count)]
        return pltpu.make_async_remote_copy(
            src_ref=rows, dst_ref=rows, send_sem=send_sems.at[n_ex + n_dp + s_idx],
            recv_sem=recv_sems.at[n_ex + n_dp + r_idx],
            device_id=(target_row * n_lo + lo, p), device_id_type=MESH)

    if bcast and n_hi == 4:
        half = n_lo // 2
        up = lax.rem(row + 1, 4)
        dn = lax.rem(row + 3, 4)
        far_row = lax.rem(row + 2, 4)
        if chain:
            for step in range(1, n_lo):
                @pl.when(lo - step >= 0)
                def _():
                    lo_copy(lo - step, lo, step, False).wait_recv()

                    @pl.when(lo < n_lo - 1)
                    def _():
                        lo_copy(lo - step, lo + 1, step, False).start()

                @pl.when(lo + step <= n_lo - 1)
                def _():
                    lo_copy(lo + step, lo, 4 + step, False).wait_recv()

                    @pl.when(lo > 0)
                    def _():
                        lo_copy(lo + step, lo - 1, 4 + step, False).start()

            @pl.when(lo < n_lo - 1)
            def _():
                lo_copy(lo, lo + 1, 0, True).wait_send()

            @pl.when(lo > 0)
            def _():
                lo_copy(lo, lo - 1, 4, True).wait_send()

            for step in range(1, n_lo):
                @pl.when((lo - step >= 0) & (lo < n_lo - 1))
                def _():
                    lo_copy(lo - step, lo + 1, step, False).wait_send()

                @pl.when((lo + step <= n_lo - 1) & (lo > 0))
                def _():
                    lo_copy(lo + step, lo - 1, 4 + step, False).wait_send()
        else:
            lax.fori_loop(1, n_lo, wait_lo, 0)
        own_dp.wait()
        to_up = fwd_copy(row * n_lo, n_lo, up, 0, row)
        to_dn = fwd_copy(row * n_lo, n_lo, dn, 1, row)
        to_up.start()
        to_dn.start()
        if split:
            lax.fori_loop(0, 6 * n_x, send_far, 0)
        else:
            lax.fori_loop(1, n_ex, send_ex, 0)
        fwd_copy(dn * n_lo, n_lo, dn, 0, dn).wait_recv()
        fwd_copy(up * n_lo, n_lo, up, 1, up).wait_recv()
        pass_up = fwd_copy(dn * n_lo, half, up, 2, 4)
        pass_dn = fwd_copy(up * n_lo + half, n_lo - half, dn, 3, 5)
        pass_up.start()
        pass_dn.start()
        lax.fori_loop(1, n_ex, wait_ex, 0)
        fwd_copy(far_row * n_lo, half, up, 2, 4).wait_recv()
        fwd_copy(far_row * n_lo + half, n_lo - half, dn, 3, 5).wait_recv()
        to_up.wait_send()
        to_dn.wait_send()
        pass_up.wait_send()
        pass_dn.wait_send()
    elif bcast:
        lax.fori_loop(1, n_lo, wait_lo, 0)
        own_dp.wait()
        lax.fori_loop(1, n_hi, send_hi, 0)
        lax.fori_loop(1, n_ex, wait_ex, 0)
        lax.fori_loop(1, n_hi, wait_hi, 0)
    else:
        lax.fori_loop(1, n_ex, wait_ex, 0)
        lax.fori_loop(1, n_dp, wait_dp, 0)
        own_dp.wait()
    own_ex.wait()


def exchange(ex_send, dp_send, bcast, cid):
    n_dp = lax.axis_size("dp")
    n_ex = lax.axis_size("expert")
    dp_block = dp_send.shape if bcast else dp_send.shape[1:]
    n_lo = 4 if n_dp % 4 == 0 else n_dp
    return pl.pallas_call(
        functools.partial(exchange_kernel, n_dp, n_ex, n_lo, bcast),
        out_shape=(
            jax.ShapeDtypeStruct(ex_send.shape, ex_send.dtype),
            jax.ShapeDtypeStruct((n_dp,) + tuple(dp_block), dp_send.dtype),
        ),
        in_specs=[pl.BlockSpec(memory_space=pl.ANY)] * 2,
        out_specs=(pl.BlockSpec(memory_space=pl.ANY), pl.BlockSpec(memory_space=pl.ANY)),
        scratch_shapes=[
            pltpu.SemaphoreType.DMA((n_ex + n_dp + n_dp,)),
            pltpu.SemaphoreType.DMA((n_ex + n_dp + n_dp,)),
            pltpu.SemaphoreType.DMA((2,)),
        ],
        compiler_params=pltpu.CompilerParams(collective_id=cid, has_side_effects=True),
    )(ex_send, dp_send)


def swiglu_forward(expert_rows, gate_up_full):
    projected = jnp.dot(expert_rows, gate_up_full, preferred_element_type=jnp.float32)
    units = gate_up_full.shape[1] // 2
    gate_part = projected[:, :units]
    up_part = projected[:, units:]
    sigmoid_gate = jax.nn.sigmoid(gate_part)
    silu_gate = gate_part * sigmoid_gate
    hidden = (silu_gate * up_part).astype(jnp.bfloat16)
    return (hidden, gate_part, up_part, sigmoid_gate, silu_gate)


def weight_blocks(grad_rows, hidden):
    product = lax.dot_general(
        grad_rows, hidden, (((0,), (0,)), ((), ())), preferred_element_type=jnp.float32
    )
    parts = lax.axis_size("dp")
    blocks = (product * loss_scale).astype(jnp.bfloat16)
    return blocks.reshape(parts, blocks.shape[0] // parts, blocks.shape[1])


def shards(tokens, out_grad, routing, gate_probs, gate_up_weight, down_weight):
    peer_count = lax.axis_size("expert")
    local_count = gate_up_weight.shape[0]
    expert_count = peer_count * local_count
    tok_rows = tokens.shape[0]
    top_count = routing.shape[1]
    model_width = tokens.shape[1]
    capacity = max(2, 9 * tok_rows * top_count // (8 * expert_count))
    pair_count = tok_rows * top_count
    slot_count = expert_count * capacity
    flat_ids = routing.reshape(pair_count)
    onehot = (flat_ids[:, None] == jnp.arange(expert_count, dtype=jnp.int32)[None, :]).astype(
        jnp.int32
    )
    slot_rank = jnp.sum((jnp.cumsum(onehot, 0) - onehot) * onehot, 1)
    slot_of_pair = flat_ids * capacity + slot_rank
    pair_index = jnp.arange(pair_count, dtype=jnp.int32)
    matches = slot_of_pair[None, :] == jnp.arange(slot_count, dtype=jnp.int32)[:, None]
    filled = jnp.any(matches, axis=1)
    source = jnp.sum(jnp.where(matches, pair_index[None, :], 0), axis=1)
    token_of_slot = source // top_count
    probs_flat = gate_probs.reshape(pair_count)
    weight_slot = jnp.where(filled, probs_flat[source], jnp.float32(0.0))
    send_rows = jnp.where(filled[:, None], tokens[token_of_slot], jnp.zeros((), jnp.bfloat16))
    send_grad = (weight_slot[:, None] * out_grad[token_of_slot].astype(jnp.float32)).astype(
        jnp.bfloat16
    )
    block_shape = (peer_count, local_count * capacity * 2 * model_width // 128, 128)
    send_both = jnp.concatenate([send_rows, send_grad], axis=1).reshape(block_shape)
    gate_width = gate_up_weight.shape[2]
    joined = jnp.concatenate([gate_up_weight[0], down_weight[0]], axis=1)
    recv_both, gathered = exchange(send_both, joined, True, 0)
    recv_both = recv_both.reshape(-1, 2 * model_width)
    expert_rows = recv_both[:, :model_width]
    grad_rows = recv_both[:, model_width:]
    full_joined = gathered.reshape(-1, joined.shape[1])
    full_gate_up = full_joined[:, :gate_width]
    full_down = full_joined[:, gate_width:]
    hidden, gate_part, up_part, sigmoid_gate, silu_gate = swiglu_forward(expert_rows, full_gate_up)
    produced = lax.dot_general(
        hidden, full_down, (((1,), (1,)), ((), ())), preferred_element_type=jnp.float32
    )
    down_parts = weight_blocks(grad_rows, hidden)
    hidden_grad = jnp.dot(grad_rows, full_down, preferred_element_type=jnp.float32)
    pre_grad = jnp.concatenate(
        [
            hidden_grad * up_part * sigmoid_gate * (1.0 + gate_part * (1.0 - sigmoid_gate)),
            hidden_grad * silu_gate,
        ],
        axis=1,
    ).astype(jnp.bfloat16)
    input_grad = lax.dot_general(
        pre_grad, full_gate_up, (((1,), (1,)), ((), ())), preferred_element_type=jnp.float32
    )
    back_both = jnp.concatenate(
        [produced.astype(jnp.bfloat16), input_grad.astype(jnp.bfloat16)], axis=1
    ).reshape(block_shape)
    returned, down_recv = exchange(back_both, down_parts, False, 1)
    chunks = model_width // 128
    pairs = returned.reshape(slot_count, 2 * chunks, 128)[slot_of_pair]
    out_pairs = pairs[:, :chunks]
    grad_pairs = pairs[:, chunks:]
    weighted = probs_flat[:, None, None] * out_pairs.astype(jnp.float32)
    mixed = jnp.sum(weighted.reshape(tok_rows, top_count, model_width), axis=1).astype(jnp.bfloat16)
    token_grad = jnp.sum(
        grad_pairs.astype(jnp.float32).reshape(tok_rows, top_count, model_width), axis=1
    ).astype(jnp.bfloat16)
    down_grad = jnp.sum(down_recv.astype(jnp.float32), axis=0)[None].astype(jnp.bfloat16)
    return (mixed, token_grad, down_grad)


def solution(mesh):
    in_specs = (
        P(("dp", "expert"), None),
        P(("dp", "expert"), None),
        P(("dp", "expert"), None),
        P(("dp", "expert"), None),
        P("expert", "dp", None),
        P("expert", "dp", None),
    )
    out_specs = (P(("dp", "expert"), None), P(("dp", "expert"), None), P("expert", "dp", None))
    return jax.shard_map(shards, mesh=mesh, in_specs=in_specs, out_specs=out_specs, check_vma=False)
```

```python
import functools

import jax
import jax.numpy as jnp
from jax import lax
from jax.experimental import pallas as pl
from jax.experimental.pallas import tpu as pltpu
from jax.sharding import PartitionSpec as P

MESH = pl.DeviceIdType.MESH

loss_scale = 0.03125


def exchange_kernel(n_dp, n_ex, n_lo, bcast, ex_send, dp_send, ex_recv, dp_recv, send_sems, recv_sems, own_sems):
    q = lax.axis_index("dp")
    p = lax.axis_index("expert")
    n_hi = n_dp // n_lo
    row = q // n_lo
    lo = q % n_lo
    barrier = pltpu.get_barrier_semaphore()
    far = n_lo == 4 and n_ex % 8 == 0

    def peer_q(j):
        if not far:
            return q
        gap = lax.rem(j // 2 - p // 2 + 8 * n_ex, 4)
        return q + (gap // 2) * (1 - gap % 2) * (3 - 2 * lo)

    def greet_ex(k, c):
        j = lax.rem(p + k, n_ex)
        pl.semaphore_signal(barrier, 1, device_id=(peer_q(j), j), device_id_type=MESH)
        return c

    def greet_dp(k, c):
        pl.semaphore_signal(barrier, 1, device_id=(lax.rem(q + k, n_dp), p), device_id_type=MESH)
        return c

    lax.fori_loop(1, n_ex, greet_ex, 0)
    lax.fori_loop(1, n_dp, greet_dp, 0)
    pl.semaphore_wait(barrier, n_ex + n_dp - 2)

    def ex_copy(j, slot):
        return pltpu.make_async_remote_copy(
            src_ref=ex_send.at[j], dst_ref=ex_recv.at[slot], send_sem=send_sems.at[j],
            recv_sem=recv_sems.at[slot], device_id=(peer_q(j), j), device_id_type=MESH)

    def dp_copy(i, slot):
        src = dp_send if bcast else dp_send.at[i]
        return pltpu.make_async_remote_copy(
            src_ref=src, dst_ref=dp_recv.at[slot], send_sem=send_sems.at[n_ex + i],
            recv_sem=recv_sems.at[n_ex + slot], device_id=(i, p), device_id_type=MESH)

    def row_copy(r, slot_row, k):
        rows = pl.ds(pl.multiple_of(slot_row * n_lo, n_lo), n_lo)
        return pltpu.make_async_remote_copy(
            src_ref=dp_recv.at[rows], dst_ref=dp_recv.at[rows],
            send_sem=send_sems.at[n_ex + n_dp + k], recv_sem=recv_sems.at[n_ex + n_dp + slot_row],
            device_id=(r * n_lo + lo, p), device_id_type=MESH)

    def send_ex(k, c):
        ex_copy(lax.rem(p + k, n_ex), p).start()
        return c

    def send_dp(k, c):
        dp_copy(lax.rem(q + k, n_dp), q).start()
        return c

    def send_lo(k, c):
        dp_copy(row * n_lo + lax.rem(lo + k, n_lo), q).start()
        return c

    own_dp = pltpu.make_async_copy(dp_send if bcast else dp_send.at[q], dp_recv.at[q], own_sems.at[1])
    chain = bcast and n_hi == 4 and n_lo == 4

    def lo_copy(origin, target, s_idx, own):
        slot = row * n_lo + origin
        return pltpu.make_async_remote_copy(
            src_ref=dp_send if own else dp_recv.at[slot], dst_ref=dp_recv.at[slot],
            send_sem=send_sems.at[n_ex + s_idx], recv_sem=recv_sems.at[n_ex + slot],
            device_id=(row * n_lo + target, p), device_id_type=MESH)

    if chain:
        @pl.when(lo < n_lo - 1)
        def _():
            lo_copy(lo, lo + 1, 0, True).start()

        @pl.when(lo > 0)
        def _():
            lo_copy(lo, lo - 1, 4, True).start()
    elif bcast:
        lax.fori_loop(1, n_lo, send_lo, 0)
    else:
        lax.fori_loop(1, n_dp, send_dp, 0)
    own_dp.start()
    own_ex = pltpu.make_async_copy(ex_send.at[p], ex_recv.at[p], own_sems.at[0])
    own_ex.start()
    late = bcast and n_hi == 4
    n_x = n_ex // 8

    def near_j(m):
        a = m // 2
        return lax.rem(p // 8 + a, n_x) * 8 + lax.rem(p // 2, 4) * 2 + lax.rem(p + m, 2)

    def far_j(m):
        b = 1 + m // (2 * n_x)
        a = (m // 2) % n_x
        return lax.rem(p // 8 + a, n_x) * 8 + lax.rem(p // 2 + b, 4) * 2 + lax.rem(p + m, 2)

    def send_near(m, c):
        ex_copy(near_j(m), p).start()
        return c

    def send_far(m, c):
        ex_copy(far_j(m), p).start()
        return c

    split = late and far
    if split:
        lax.fori_loop(1, 2 * n_x, send_near, 0)
    elif not late:
        lax.fori_loop(1, n_ex, send_ex, 0)

    def wait_ex(k, c):
        j = lax.rem(p + k, n_ex)
        ex_copy(j, p).wait_send()
        ex_copy(j, j).wait_recv()
        return c

    def wait_dp(k, c):
        i = lax.rem(q + k, n_dp)
        dp_copy(i, q).wait_send()
        dp_copy(i, i).wait_recv()
        return c

    def wait_lo(k, c):
        i = row * n_lo + lax.rem(lo + k, n_lo)
        dp_copy(i, q).wait_send()
        dp_copy(i, i).wait_recv()
        return c

    def send_hi(k, c):
        row_copy(lax.rem(row + k, n_hi), row, k).start()
        return c

    def wait_hi(k, c):
        r = lax.rem(row + k, n_hi)
        row_copy(r, row, k).wait_send()
        row_copy(r, r, k).wait_recv()
        return c

    def fwd_copy(start, count, target_row, s_idx, r_idx):
        rows = dp_recv.at[pl.ds(start, count)]
        return pltpu.make_async_remote_copy(
            src_ref=rows, dst_ref=rows, send_sem=send_sems.at[n_ex + n_dp + s_idx],
            recv_sem=recv_sems.at[n_ex + n_dp + r_idx],
            device_id=(target_row * n_lo + lo, p), device_id_type=MESH)

    if bcast and n_hi == 4:
        half = n_lo // 2
        up = lax.rem(row + 1, 4)
        dn = lax.rem(row + 3, 4)
        far_row = lax.rem(row + 2, 4)
        if chain:
            for step in range(1, n_lo):
                @pl.when(lo - step >= 0)
                def _():
                    lo_copy(lo - step, lo, step, False).wait_recv()

                    @pl.when(lo < n_lo - 1)
                    def _():
                        lo_copy(lo - step, lo + 1, step, False).start()

                @pl.when(lo + step <= n_lo - 1)
                def _():
                    lo_copy(lo + step, lo, 4 + step, False).wait_recv()

                    @pl.when(lo > 0)
                    def _():
                        lo_copy(lo + step, lo - 1, 4 + step, False).start()

            @pl.when(lo < n_lo - 1)
            def _():
                lo_copy(lo, lo + 1, 0, True).wait_send()

            @pl.when(lo > 0)
            def _():
                lo_copy(lo, lo - 1, 4, True).wait_send()

            for step in range(1, n_lo):
                @pl.when((lo - step >= 0) & (lo < n_lo - 1))
                def _():
                    lo_copy(lo - step, lo + 1, step, False).wait_send()

                @pl.when((lo + step <= n_lo - 1) & (lo > 0))
                def _():
                    lo_copy(lo + step, lo - 1, 4 + step, False).wait_send()
        else:
            lax.fori_loop(1, n_lo, wait_lo, 0)
        own_dp.wait()
        to_up = fwd_copy(row * n_lo, n_lo, up, 0, row)
        to_dn = fwd_copy(row * n_lo, n_lo, dn, 1, row)
        to_up.start()
        to_dn.start()
        if split:
            lax.fori_loop(0, 6 * n_x, send_far, 0)
        else:
            lax.fori_loop(1, n_ex, send_ex, 0)
        fwd_copy(dn * n_lo, n_lo, dn, 0, dn).wait_recv()
        fwd_copy(up * n_lo, n_lo, up, 1, up).wait_recv()
        pass_up = fwd_copy(dn * n_lo, half, up, 2, 4)
        pass_dn = fwd_copy(up * n_lo + half, n_lo - half, dn, 3, 5)
        pass_up.start()
        pass_dn.start()
        lax.fori_loop(1, n_ex, wait_ex, 0)
        fwd_copy(far_row * n_lo, half, up, 2, 4).wait_recv()
        fwd_copy(far_row * n_lo + half, n_lo - half, dn, 3, 5).wait_recv()
        to_up.wait_send()
        to_dn.wait_send()
        pass_up.wait_send()
        pass_dn.wait_send()
    elif bcast:
        lax.fori_loop(1, n_lo, wait_lo, 0)
        own_dp.wait()
        lax.fori_loop(1, n_hi, send_hi, 0)
        lax.fori_loop(1, n_ex, wait_ex, 0)
        lax.fori_loop(1, n_hi, wait_hi, 0)
    else:
        lax.fori_loop(1, n_ex, wait_ex, 0)
        lax.fori_loop(1, n_dp, wait_dp, 0)
        own_dp.wait()
    own_ex.wait()


def exchange(ex_send, dp_send, bcast, cid):
    n_dp = lax.axis_size("dp")
    n_ex = lax.axis_size("expert")
    dp_block = dp_send.shape if bcast else dp_send.shape[1:]
    n_lo = 4 if n_dp % 4 == 0 else n_dp
    return pl.pallas_call(
        functools.partial(exchange_kernel, n_dp, n_ex, n_lo, bcast),
        out_shape=(
            jax.ShapeDtypeStruct(ex_send.shape, ex_send.dtype),
            jax.ShapeDtypeStruct((n_dp,) + tuple(dp_block), dp_send.dtype),
        ),
        in_specs=[pl.BlockSpec(memory_space=pl.ANY)] * 2,
        out_specs=(pl.BlockSpec(memory_space=pl.ANY), pl.BlockSpec(memory_space=pl.ANY)),
        scratch_shapes=[
            pltpu.SemaphoreType.DMA((n_ex + n_dp + n_dp,)),
            pltpu.SemaphoreType.DMA((n_ex + n_dp + n_dp,)),
            pltpu.SemaphoreType.DMA((2,)),
        ],
        compiler_params=pltpu.CompilerParams(collective_id=cid, has_side_effects=True),
    )(ex_send, dp_send)


def swiglu_forward(expert_rows, gate_up_full):
    projected = jnp.dot(expert_rows, gate_up_full, preferred_element_type=jnp.float32)
    units = gate_up_full.shape[1] // 2
    gate_part = projected[:, :units]
    up_part = projected[:, units:]
    sigmoid_gate = jax.nn.sigmoid(gate_part)
    silu_gate = gate_part * sigmoid_gate
    hidden = (silu_gate * up_part).astype(jnp.bfloat16)
    return (hidden, gate_part, up_part, sigmoid_gate, silu_gate)


def weight_blocks(grad_rows, hidden):
    product = lax.dot_general(
        grad_rows, hidden, (((0,), (0,)), ((), ())), preferred_element_type=jnp.float32
    )
    parts = lax.axis_size("dp")
    blocks = (product * loss_scale).astype(jnp.bfloat16)
    return blocks.reshape(parts, blocks.shape[0] // parts, blocks.shape[1])


def shards(tokens, out_grad, routing, gate_probs, gate_up_weight, down_weight):
    peer_count = lax.axis_size("expert")
    local_count = gate_up_weight.shape[0]
    expert_count = peer_count * local_count
    tok_rows = tokens.shape[0]
    top_count = routing.shape[1]
    model_width = tokens.shape[1]
    capacity = max(2, 9 * tok_rows * top_count // (8 * expert_count))
    pair_count = tok_rows * top_count
    slot_count = expert_count * capacity
    flat_ids = routing.reshape(pair_count)
    onehot = (flat_ids[:, None] == jnp.arange(expert_count, dtype=jnp.int32)[None, :]).astype(
        jnp.int32
    )
    slot_rank = jnp.sum((jnp.cumsum(onehot, 0) - onehot) * onehot, 1)
    slot_of_pair = flat_ids * capacity + slot_rank
    pair_index = jnp.arange(pair_count, dtype=jnp.int32)
    matches = slot_of_pair[None, :] == jnp.arange(slot_count, dtype=jnp.int32)[:, None]
    filled = jnp.any(matches, axis=1)
    source = jnp.sum(jnp.where(matches, pair_index[None, :], 0), axis=1)
    token_of_slot = source // top_count
    probs_flat = gate_probs.reshape(pair_count)
    weight_slot = jnp.where(filled, probs_flat[source], jnp.float32(0.0))
    chunks = model_width // 128
    tok_chunks = tokens.reshape(tok_rows, chunks, 128)
    grad_chunks = out_grad.reshape(tok_rows, chunks, 128)
    send_rows = jnp.where(
        filled[:, None, None], tok_chunks[token_of_slot], jnp.zeros((), jnp.bfloat16)
    )
    send_grad = (
        weight_slot[:, None, None] * grad_chunks[token_of_slot].astype(jnp.float32)
    ).astype(jnp.bfloat16)
    block_shape = (peer_count, local_count * capacity * 2 * model_width // 128, 128)
    send_both = jnp.concatenate([send_rows, send_grad], axis=1).reshape(block_shape)
    gate_width = gate_up_weight.shape[2]
    joined = jnp.concatenate([gate_up_weight[0], down_weight[0]], axis=1)
    recv_both, gathered = exchange(send_both, joined, True, 0)
    recv_both = recv_both.reshape(-1, 2 * model_width)
    expert_rows = recv_both[:, :model_width]
    grad_rows = recv_both[:, model_width:]
    full_joined = gathered.reshape(-1, joined.shape[1])
    full_gate_up = full_joined[:, :gate_width]
    full_down = full_joined[:, gate_width:]
    hidden, gate_part, up_part, sigmoid_gate, silu_gate = swiglu_forward(expert_rows, full_gate_up)
    produced = lax.dot_general(
        hidden, full_down, (((1,), (1,)), ((), ())), preferred_element_type=jnp.float32
    )
    down_parts = weight_blocks(grad_rows, hidden)
    hidden_grad = jnp.dot(grad_rows, full_down, preferred_element_type=jnp.float32)
    pre_grad = jnp.concatenate(
        [
            hidden_grad * up_part * sigmoid_gate * (1.0 + gate_part * (1.0 - sigmoid_gate)),
            hidden_grad * silu_gate,
        ],
        axis=1,
    ).astype(jnp.bfloat16)
    input_grad = lax.dot_general(
        pre_grad, full_gate_up, (((1,), (1,)), ((), ())), preferred_element_type=jnp.float32
    )
    back_both = jnp.concatenate(
        [
            produced.astype(jnp.bfloat16).reshape(slot_count, chunks, 128),
            input_grad.astype(jnp.bfloat16).reshape(slot_count, chunks, 128),
        ],
        axis=1,
    ).reshape(block_shape)
    returned, down_recv = exchange(back_both, down_parts, False, 1)
    pairs = returned.reshape(slot_count, 2 * chunks, 128)[slot_of_pair]
    out_pairs = pairs[:, :chunks]
    grad_pairs = pairs[:, chunks:]
    weighted = probs_flat[:, None, None] * out_pairs.astype(jnp.float32)
    mixed = jnp.sum(weighted.reshape(tok_rows, top_count, model_width), axis=1).astype(jnp.bfloat16)
    token_grad = jnp.sum(
        grad_pairs.astype(jnp.float32).reshape(tok_rows, top_count, model_width), axis=1
    ).astype(jnp.bfloat16)
    down_grad = jnp.sum(down_recv.astype(jnp.float32), axis=0)[None].astype(jnp.bfloat16)
    return (mixed, token_grad, down_grad)


def solution(mesh):
    in_specs = (
        P(("dp", "expert"), None),
        P(("dp", "expert"), None),
        P(("dp", "expert"), None),
        P(("dp", "expert"), None),
        P("expert", "dp", None),
        P("expert", "dp", None),
    )
    out_specs = (P(("dp", "expert"), None), P(("dp", "expert"), None), P("expert", "dp", None))
    return jax.shard_map(shards, mesh=mesh, in_specs=in_specs, out_specs=out_specs, check_vma=False)
```

```python
import functools

import jax
import jax.numpy as jnp
from jax import lax
from jax.experimental import pallas as pl
from jax.experimental.pallas import tpu as pltpu
from jax.sharding import PartitionSpec as P

MESH = pl.DeviceIdType.MESH

loss_scale = 0.03125


def exchange_kernel(n_dp, n_ex, n_lo, bcast, ex_send, dp_send, ex_recv, dp_recv, send_sems, recv_sems, own_sems):
    q = lax.axis_index("dp")
    p = lax.axis_index("expert")
    n_hi = n_dp // n_lo
    row = q // n_lo
    lo = q % n_lo
    barrier = pltpu.get_barrier_semaphore()
    far = n_lo == 4 and n_ex % 8 == 0

    def peer_q(j):
        if not far:
            return q
        gap = lax.rem(j // 2 - p // 2 + 8 * n_ex, 4)
        return q + (gap // 2) * (1 - gap % 2) * (3 - 2 * lo)

    def greet_ex(k, c):
        j = lax.rem(p + k, n_ex)
        pl.semaphore_signal(barrier, 1, device_id=(peer_q(j), j), device_id_type=MESH)
        return c

    def greet_dp(k, c):
        pl.semaphore_signal(barrier, 1, device_id=(lax.rem(q + k, n_dp), p), device_id_type=MESH)
        return c

    lax.fori_loop(1, n_ex, greet_ex, 0)
    lax.fori_loop(1, n_dp, greet_dp, 0)
    pl.semaphore_wait(barrier, n_ex + n_dp - 2)

    def ex_copy(j, slot):
        return pltpu.make_async_remote_copy(
            src_ref=ex_send.at[j], dst_ref=ex_recv.at[slot], send_sem=send_sems.at[j],
            recv_sem=recv_sems.at[slot], device_id=(peer_q(j), j), device_id_type=MESH)

    def dp_copy(i, slot):
        src = dp_send if bcast else dp_send.at[i]
        return pltpu.make_async_remote_copy(
            src_ref=src, dst_ref=dp_recv.at[slot], send_sem=send_sems.at[n_ex + i],
            recv_sem=recv_sems.at[n_ex + slot], device_id=(i, p), device_id_type=MESH)

    def row_copy(r, slot_row, k):
        rows = pl.ds(pl.multiple_of(slot_row * n_lo, n_lo), n_lo)
        return pltpu.make_async_remote_copy(
            src_ref=dp_recv.at[rows], dst_ref=dp_recv.at[rows],
            send_sem=send_sems.at[n_ex + n_dp + k], recv_sem=recv_sems.at[n_ex + n_dp + slot_row],
            device_id=(r * n_lo + lo, p), device_id_type=MESH)

    def send_ex(k, c):
        ex_copy(lax.rem(p + k, n_ex), p).start()
        return c

    def send_dp(k, c):
        dp_copy(lax.rem(q + k, n_dp), q).start()
        return c

    def send_lo(k, c):
        dp_copy(row * n_lo + lax.rem(lo + k, n_lo), q).start()
        return c

    own_dp = pltpu.make_async_copy(dp_send if bcast else dp_send.at[q], dp_recv.at[q], own_sems.at[1])
    chain = bcast and n_hi == 4 and n_lo == 4

    def lo_copy(origin, target, s_idx, own):
        slot = row * n_lo + origin
        return pltpu.make_async_remote_copy(
            src_ref=dp_send if own else dp_recv.at[slot], dst_ref=dp_recv.at[slot],
            send_sem=send_sems.at[n_ex + s_idx], recv_sem=recv_sems.at[n_ex + slot],
            device_id=(row * n_lo + target, p), device_id_type=MESH)

    if chain:
        @pl.when(lo < n_lo - 1)
        def _():
            lo_copy(lo, lo + 1, 0, True).start()

        @pl.when(lo > 0)
        def _():
            lo_copy(lo, lo - 1, 4, True).start()
    elif bcast:
        lax.fori_loop(1, n_lo, send_lo, 0)
    else:
        lax.fori_loop(1, n_dp, send_dp, 0)
    own_dp.start()
    own_ex = pltpu.make_async_copy(ex_send.at[p], ex_recv.at[p], own_sems.at[0])
    own_ex.start()
    late = bcast and n_hi == 4
    n_x = n_ex // 8

    def near_j(m):
        a = m // 2
        return lax.rem(p // 8 + a, n_x) * 8 + lax.rem(p // 2, 4) * 2 + lax.rem(p + m, 2)

    def far_j(m):
        b = 1 + m // (2 * n_x)
        a = (m // 2) % n_x
        return lax.rem(p // 8 + a, n_x) * 8 + lax.rem(p // 2 + b, 4) * 2 + lax.rem(p + m, 2)

    def send_near(m, c):
        ex_copy(near_j(m), p).start()
        return c

    def send_far(m, c):
        ex_copy(far_j(m), p).start()
        return c

    split = late and far
    if split:
        lax.fori_loop(1, 2 * n_x, send_near, 0)
    elif not late:
        lax.fori_loop(1, n_ex, send_ex, 0)

    def wait_ex(k, c):
        j = lax.rem(p + k, n_ex)
        ex_copy(j, p).wait_send()
        ex_copy(j, j).wait_recv()
        return c

    def wait_dp(k, c):
        i = lax.rem(q + k, n_dp)
        dp_copy(i, q).wait_send()
        dp_copy(i, i).wait_recv()
        return c

    def wait_lo(k, c):
        i = row * n_lo + lax.rem(lo + k, n_lo)
        dp_copy(i, q).wait_send()
        dp_copy(i, i).wait_recv()
        return c

    def send_hi(k, c):
        row_copy(lax.rem(row + k, n_hi), row, k).start()
        return c

    def wait_hi(k, c):
        r = lax.rem(row + k, n_hi)
        row_copy(r, row, k).wait_send()
        row_copy(r, r, k).wait_recv()
        return c

    def fwd_copy(start, count, target_row, s_idx, r_idx):
        rows = dp_recv.at[pl.ds(start, count)]
        return pltpu.make_async_remote_copy(
            src_ref=rows, dst_ref=rows, send_sem=send_sems.at[n_ex + n_dp + s_idx],
            recv_sem=recv_sems.at[n_ex + n_dp + r_idx],
            device_id=(target_row * n_lo + lo, p), device_id_type=MESH)

    if bcast and n_hi == 4:
        half = n_lo // 2
        up = lax.rem(row + 1, 4)
        dn = lax.rem(row + 3, 4)
        far_row = lax.rem(row + 2, 4)
        if chain:
            for step in range(1, n_lo):
                @pl.when(lo - step >= 0)
                def _():
                    lo_copy(lo - step, lo, step, False).wait_recv()

                    @pl.when(lo < n_lo - 1)
                    def _():
                        lo_copy(lo - step, lo + 1, step, False).start()

                @pl.when(lo + step <= n_lo - 1)
                def _():
                    lo_copy(lo + step, lo, 4 + step, False).wait_recv()

                    @pl.when(lo > 0)
                    def _():
                        lo_copy(lo + step, lo - 1, 4 + step, False).start()

            @pl.when(lo < n_lo - 1)
            def _():
                lo_copy(lo, lo + 1, 0, True).wait_send()

            @pl.when(lo > 0)
            def _():
                lo_copy(lo, lo - 1, 4, True).wait_send()

            for step in range(1, n_lo):
                @pl.when((lo - step >= 0) & (lo < n_lo - 1))
                def _():
                    lo_copy(lo - step, lo + 1, step, False).wait_send()

                @pl.when((lo + step <= n_lo - 1) & (lo > 0))
                def _():
                    lo_copy(lo + step, lo - 1, 4 + step, False).wait_send()
        else:
            lax.fori_loop(1, n_lo, wait_lo, 0)
        own_dp.wait()
        to_up = fwd_copy(row * n_lo, n_lo, up, 0, row)
        to_dn = fwd_copy(row * n_lo, n_lo, dn, 1, row)
        to_up.start()
        to_dn.start()
        if split:
            lax.fori_loop(0, 6 * n_x, send_far, 0)
        else:
            lax.fori_loop(1, n_ex, send_ex, 0)
        fwd_copy(dn * n_lo, n_lo, dn, 0, dn).wait_recv()
        fwd_copy(up * n_lo, n_lo, up, 1, up).wait_recv()
        pass_up = fwd_copy(dn * n_lo, half, up, 2, 4)
        pass_dn = fwd_copy(up * n_lo + half, n_lo - half, dn, 3, 5)
        pass_up.start()
        pass_dn.start()
        lax.fori_loop(1, n_ex, wait_ex, 0)
        fwd_copy(far_row * n_lo, half, up, 2, 4).wait_recv()
        fwd_copy(far_row * n_lo + half, n_lo - half, dn, 3, 5).wait_recv()
        to_up.wait_send()
        to_dn.wait_send()
        pass_up.wait_send()
        pass_dn.wait_send()
    elif bcast:
        lax.fori_loop(1, n_lo, wait_lo, 0)
        own_dp.wait()
        lax.fori_loop(1, n_hi, send_hi, 0)
        lax.fori_loop(1, n_ex, wait_ex, 0)
        lax.fori_loop(1, n_hi, wait_hi, 0)
    else:
        lax.fori_loop(1, n_ex, wait_ex, 0)
        lax.fori_loop(1, n_dp, wait_dp, 0)
        own_dp.wait()
    own_ex.wait()


def exchange(ex_send, dp_send, bcast, cid):
    n_dp = lax.axis_size("dp")
    n_ex = lax.axis_size("expert")
    dp_block = dp_send.shape if bcast else dp_send.shape[1:]
    n_lo = 4 if n_dp % 4 == 0 else n_dp
    return pl.pallas_call(
        functools.partial(exchange_kernel, n_dp, n_ex, n_lo, bcast),
        out_shape=(
            jax.ShapeDtypeStruct(ex_send.shape, ex_send.dtype),
            jax.ShapeDtypeStruct((n_dp,) + tuple(dp_block), dp_send.dtype),
        ),
        in_specs=[pl.BlockSpec(memory_space=pl.ANY)] * 2,
        out_specs=(pl.BlockSpec(memory_space=pl.ANY), pl.BlockSpec(memory_space=pl.ANY)),
        scratch_shapes=[
            pltpu.SemaphoreType.DMA((n_ex + n_dp + n_dp,)),
            pltpu.SemaphoreType.DMA((n_ex + n_dp + n_dp,)),
            pltpu.SemaphoreType.DMA((2,)),
        ],
        compiler_params=pltpu.CompilerParams(collective_id=cid, has_side_effects=True),
    )(ex_send, dp_send)


def swiglu_forward(expert_rows, gate_up_full):
    projected = lax.dot_general(
        expert_rows,
        gate_up_full.reshape(expert_rows.shape[1], expert_rows.shape[2], -1),
        (((1, 2), (0, 1)), ((), ())),
        preferred_element_type=jnp.float32,
    )
    units = gate_up_full.shape[1] // 2
    gate_part = projected[:, :units]
    up_part = projected[:, units:]
    sigmoid_gate = jax.nn.sigmoid(gate_part)
    silu_gate = gate_part * sigmoid_gate
    hidden = (silu_gate * up_part).astype(jnp.bfloat16)
    return (hidden, gate_part, up_part, sigmoid_gate, silu_gate)


def weight_blocks(grad_rows, hidden):
    product = lax.dot_general(
        grad_rows, hidden, (((0,), (0,)), ((), ())), preferred_element_type=jnp.float32
    )
    parts = lax.axis_size("dp")
    blocks = (product * loss_scale).astype(jnp.bfloat16).reshape(-1, hidden.shape[1])
    return blocks.reshape(parts, blocks.shape[0] // parts, blocks.shape[1])


def shards(tokens, out_grad, routing, gate_probs, gate_up_weight, down_weight):
    peer_count = lax.axis_size("expert")
    local_count = gate_up_weight.shape[0]
    expert_count = peer_count * local_count
    tok_rows = tokens.shape[0]
    top_count = routing.shape[1]
    model_width = tokens.shape[1]
    capacity = max(2, 9 * tok_rows * top_count // (8 * expert_count))
    pair_count = tok_rows * top_count
    slot_count = expert_count * capacity
    flat_ids = routing.reshape(pair_count)
    onehot = (flat_ids[:, None] == jnp.arange(expert_count, dtype=jnp.int32)[None, :]).astype(
        jnp.int32
    )
    slot_rank = jnp.sum((jnp.cumsum(onehot, 0) - onehot) * onehot, 1)
    slot_of_pair = flat_ids * capacity + slot_rank
    pair_index = jnp.arange(pair_count, dtype=jnp.int32)
    matches = slot_of_pair[None, :] == jnp.arange(slot_count, dtype=jnp.int32)[:, None]
    filled = jnp.any(matches, axis=1)
    source = jnp.sum(jnp.where(matches, pair_index[None, :], 0), axis=1)
    token_of_slot = source // top_count
    probs_flat = gate_probs.reshape(pair_count)
    weight_slot = jnp.where(filled, probs_flat[source], jnp.float32(0.0))
    chunks = model_width // 128
    tok_chunks = tokens.reshape(tok_rows, chunks, 128)
    grad_chunks = out_grad.reshape(tok_rows, chunks, 128)
    send_rows = jnp.where(
        filled[:, None, None], tok_chunks[token_of_slot], jnp.zeros((), jnp.bfloat16)
    )
    send_grad = (
        weight_slot[:, None, None] * grad_chunks[token_of_slot].astype(jnp.float32)
    ).astype(jnp.bfloat16)
    block_shape = (peer_count, local_count * capacity * 2 * model_width // 128, 128)
    send_both = jnp.concatenate([send_rows, send_grad], axis=1).reshape(block_shape)
    gate_width = gate_up_weight.shape[2]
    joined = jnp.concatenate([gate_up_weight[0], down_weight[0]], axis=1)
    recv_both, gathered = exchange(send_both, joined, True, 0)
    recv_both = recv_both.reshape(slot_count, 2 * chunks, 128)
    expert_rows = recv_both[:, :chunks]
    grad_rows = recv_both[:, chunks:]
    full_joined = gathered.reshape(-1, joined.shape[1])
    full_gate_up = full_joined[:, :gate_width]
    full_down = full_joined[:, gate_width:]
    hidden, gate_part, up_part, sigmoid_gate, silu_gate = swiglu_forward(expert_rows, full_gate_up)
    produced = lax.dot_general(
        hidden, full_down, (((1,), (1,)), ((), ())), preferred_element_type=jnp.float32
    )
    down_parts = weight_blocks(grad_rows, hidden)
    hidden_grad = lax.dot_general(
        grad_rows,
        full_down.reshape(chunks, 128, -1),
        (((1, 2), (0, 1)), ((), ())),
        preferred_element_type=jnp.float32,
    )
    pre_grad = jnp.concatenate(
        [
            hidden_grad * up_part * sigmoid_gate * (1.0 + gate_part * (1.0 - sigmoid_gate)),
            hidden_grad * silu_gate,
        ],
        axis=1,
    ).astype(jnp.bfloat16)
    input_grad = lax.dot_general(
        pre_grad, full_gate_up, (((1,), (1,)), ((), ())), preferred_element_type=jnp.float32
    )
    back_both = jnp.concatenate(
        [
            produced.astype(jnp.bfloat16).reshape(slot_count, chunks, 128),
            input_grad.astype(jnp.bfloat16).reshape(slot_count, chunks, 128),
        ],
        axis=1,
    ).reshape(block_shape)
    returned, down_recv = exchange(back_both, down_parts, False, 1)
    pairs = returned.reshape(slot_count, 2 * chunks, 128)[slot_of_pair]
    out_pairs = pairs[:, :chunks]
    grad_pairs = pairs[:, chunks:]
    weighted = probs_flat[:, None, None] * out_pairs.astype(jnp.float32)
    mixed = jnp.sum(weighted.reshape(tok_rows, top_count, model_width), axis=1).astype(jnp.bfloat16)
    token_grad = jnp.sum(
        grad_pairs.astype(jnp.float32).reshape(tok_rows, top_count, model_width), axis=1
    ).astype(jnp.bfloat16)
    down_grad = jnp.sum(down_recv.astype(jnp.float32), axis=0)[None].astype(jnp.bfloat16)
    return (mixed, token_grad, down_grad)


def solution(mesh):
    in_specs = (
        P(("dp", "expert"), None),
        P(("dp", "expert"), None),
        P(("dp", "expert"), None),
        P(("dp", "expert"), None),
        P("expert", "dp", None),
        P("expert", "dp", None),
    )
    out_specs = (P(("dp", "expert"), None), P(("dp", "expert"), None), P("expert", "dp", None))
    return jax.shard_map(shards, mesh=mesh, in_specs=in_specs, out_specs=out_specs, check_vma=False)
```

```python
import functools

import jax
import jax.numpy as jnp
from jax import lax
from jax.experimental import pallas as pl
from jax.experimental.pallas import tpu as pltpu
from jax.sharding import PartitionSpec as P

MESH = pl.DeviceIdType.MESH

loss_scale = 0.03125


def exchange_kernel(n_dp, n_ex, n_lo, bcast, ex_send, dp_send, ex_recv, dp_recv, send_sems, recv_sems, own_sems):
    q = lax.axis_index("dp")
    p = lax.axis_index("expert")
    n_hi = n_dp // n_lo
    row = q // n_lo
    lo = q % n_lo
    barrier = pltpu.get_barrier_semaphore()
    far = n_lo == 4 and n_ex % 8 == 0

    def peer_q(j):
        if not far:
            return q
        gap = lax.rem(j // 2 - p // 2 + 8 * n_ex, 4)
        return q + (gap // 2) * (1 - gap % 2) * (3 - 2 * lo)

    def greet_ex(k, c):
        j = lax.rem(p + k, n_ex)
        pl.semaphore_signal(barrier, 1, device_id=(peer_q(j), j), device_id_type=MESH)
        return c

    def greet_dp(k, c):
        pl.semaphore_signal(barrier, 1, device_id=(lax.rem(q + k, n_dp), p), device_id_type=MESH)
        return c

    lax.fori_loop(1, n_ex, greet_ex, 0)
    lax.fori_loop(1, n_dp, greet_dp, 0)
    pl.semaphore_wait(barrier, n_ex + n_dp - 2)

    def ex_copy(j, slot):
        return pltpu.make_async_remote_copy(
            src_ref=ex_send.at[j], dst_ref=ex_recv.at[slot], send_sem=send_sems.at[j],
            recv_sem=recv_sems.at[slot], device_id=(peer_q(j), j), device_id_type=MESH)

    def dp_copy(i, slot):
        src = dp_send if bcast else dp_send.at[i]
        return pltpu.make_async_remote_copy(
            src_ref=src, dst_ref=dp_recv.at[slot], send_sem=send_sems.at[n_ex + i],
            recv_sem=recv_sems.at[n_ex + slot], device_id=(i, p), device_id_type=MESH)

    def row_copy(r, slot_row, k):
        rows = pl.ds(pl.multiple_of(slot_row * n_lo, n_lo), n_lo)
        return pltpu.make_async_remote_copy(
            src_ref=dp_recv.at[rows], dst_ref=dp_recv.at[rows],
            send_sem=send_sems.at[n_ex + n_dp + k], recv_sem=recv_sems.at[n_ex + n_dp + slot_row],
            device_id=(r * n_lo + lo, p), device_id_type=MESH)

    def send_ex(k, c):
        ex_copy(lax.rem(p + k, n_ex), p).start()
        return c

    def send_dp(k, c):
        dp_copy(lax.rem(q + k, n_dp), q).start()
        return c

    def send_lo(k, c):
        dp_copy(row * n_lo + lax.rem(lo + k, n_lo), q).start()
        return c

    own_dp = pltpu.make_async_copy(dp_send if bcast else dp_send.at[q], dp_recv.at[q], own_sems.at[1])
    own_dp.start()
    chain = bcast and n_hi == 4 and n_lo == 4

    def lo_copy(origin, target, s_idx, own):
        slot = row * n_lo + origin
        return pltpu.make_async_remote_copy(
            src_ref=dp_send if own else dp_recv.at[slot], dst_ref=dp_recv.at[slot],
            send_sem=send_sems.at[n_ex + s_idx], recv_sem=recv_sems.at[n_ex + slot],
            device_id=(row * n_lo + target, p), device_id_type=MESH)

    if chain:
        @pl.when(lo < n_lo - 1)
        def _():
            lo_copy(lo, lo + 1, 0, True).start()

        @pl.when(lo > 0)
        def _():
            lo_copy(lo, lo - 1, 4, True).start()
    elif bcast:
        lax.fori_loop(1, n_lo, send_lo, 0)
    else:
        lax.fori_loop(1, n_dp, send_dp, 0)
    own_ex = pltpu.make_async_copy(ex_send.at[p], ex_recv.at[p], own_sems.at[0])
    own_ex.start()
    late = bcast and n_hi == 4
    n_x = n_ex // 8

    def near_j(m):
        a = m // 2
        return lax.rem(p // 8 + a, n_x) * 8 + lax.rem(p // 2, 4) * 2 + lax.rem(p + m, 2)

    def far_j(m):
        b = 1 + m // (2 * n_x)
        a = (m // 2) % n_x
        return lax.rem(p // 8 + a, n_x) * 8 + lax.rem(p // 2 + b, 4) * 2 + lax.rem(p + m, 2)

    def send_near(m, c):
        ex_copy(near_j(m), p).start()
        return c

    def send_far(m, c):
        ex_copy(far_j(m), p).start()
        return c

    split = late and far
    if split:
        lax.fori_loop(1, 2 * n_x, send_near, 0)
    elif not late:
        lax.fori_loop(1, n_ex, send_ex, 0)

    def wait_ex(k, c):
        j = lax.rem(p + k, n_ex)
        ex_copy(j, p).wait_send()
        ex_copy(j, j).wait_recv()
        return c

    def wait_dp(k, c):
        i = lax.rem(q + k, n_dp)
        dp_copy(i, q).wait_send()
        dp_copy(i, i).wait_recv()
        return c

    def wait_lo(k, c):
        i = row * n_lo + lax.rem(lo + k, n_lo)
        dp_copy(i, q).wait_send()
        dp_copy(i, i).wait_recv()
        return c

    def send_hi(k, c):
        row_copy(lax.rem(row + k, n_hi), row, k).start()
        return c

    def wait_hi(k, c):
        r = lax.rem(row + k, n_hi)
        row_copy(r, row, k).wait_send()
        row_copy(r, r, k).wait_recv()
        return c

    def fwd_copy(start, count, target_row, s_idx, r_idx):
        rows = dp_recv.at[pl.ds(start, count)]
        return pltpu.make_async_remote_copy(
            src_ref=rows, dst_ref=rows, send_sem=send_sems.at[n_ex + n_dp + s_idx],
            recv_sem=recv_sems.at[n_ex + n_dp + r_idx],
            device_id=(target_row * n_lo + lo, p), device_id_type=MESH)

    if bcast and n_hi == 4:
        half = n_lo // 2
        up = lax.rem(row + 1, 4)
        dn = lax.rem(row + 3, 4)
        far_row = lax.rem(row + 2, 4)
        if chain:
            for step in range(1, n_lo):
                @pl.when(lo - step >= 0)
                def _():
                    lo_copy(lo - step, lo, step, False).wait_recv()

                    @pl.when(lo < n_lo - 1)
                    def _():
                        lo_copy(lo - step, lo + 1, step, False).start()

                @pl.when(lo + step <= n_lo - 1)
                def _():
                    lo_copy(lo + step, lo, 4 + step, False).wait_recv()

                    @pl.when(lo > 0)
                    def _():
                        lo_copy(lo + step, lo - 1, 4 + step, False).start()

            @pl.when(lo < n_lo - 1)
            def _():
                lo_copy(lo, lo + 1, 0, True).wait_send()

            @pl.when(lo > 0)
            def _():
                lo_copy(lo, lo - 1, 4, True).wait_send()

            for step in range(1, n_lo):
                @pl.when((lo - step >= 0) & (lo < n_lo - 1))
                def _():
                    lo_copy(lo - step, lo + 1, step, False).wait_send()

                @pl.when((lo + step <= n_lo - 1) & (lo > 0))
                def _():
                    lo_copy(lo + step, lo - 1, 4 + step, False).wait_send()
        else:
            lax.fori_loop(1, n_lo, wait_lo, 0)
        own_dp.wait()
        to_up = fwd_copy(row * n_lo, n_lo, up, 0, row)
        to_dn = fwd_copy(row * n_lo, n_lo, dn, 1, row)
        to_up.start()
        to_dn.start()
        if split:
            lax.fori_loop(0, 6 * n_x, send_far, 0)
        else:
            lax.fori_loop(1, n_ex, send_ex, 0)
        fwd_copy(dn * n_lo, n_lo, dn, 0, dn).wait_recv()
        fwd_copy(up * n_lo, n_lo, up, 1, up).wait_recv()
        pass_up = fwd_copy(dn * n_lo, half, up, 2, 4)
        pass_dn = fwd_copy(up * n_lo + half, n_lo - half, dn, 3, 5)
        pass_up.start()
        pass_dn.start()
        lax.fori_loop(1, n_ex, wait_ex, 0)
        fwd_copy(far_row * n_lo, half, up, 2, 4).wait_recv()
        fwd_copy(far_row * n_lo + half, n_lo - half, dn, 3, 5).wait_recv()
        to_up.wait_send()
        to_dn.wait_send()
        pass_up.wait_send()
        pass_dn.wait_send()
    elif bcast:
        lax.fori_loop(1, n_lo, wait_lo, 0)
        own_dp.wait()
        lax.fori_loop(1, n_hi, send_hi, 0)
        lax.fori_loop(1, n_ex, wait_ex, 0)
        lax.fori_loop(1, n_hi, wait_hi, 0)
    else:
        lax.fori_loop(1, n_ex, wait_ex, 0)
        lax.fori_loop(1, n_dp, wait_dp, 0)
        own_dp.wait()
    own_ex.wait()


def exchange(ex_send, dp_send, bcast, cid):
    n_dp = lax.axis_size("dp")
    n_ex = lax.axis_size("expert")
    dp_block = dp_send.shape if bcast else dp_send.shape[1:]
    n_lo = 4 if n_dp % 4 == 0 else n_dp
    return pl.pallas_call(
        functools.partial(exchange_kernel, n_dp, n_ex, n_lo, bcast),
        out_shape=(
            jax.ShapeDtypeStruct(ex_send.shape, ex_send.dtype),
            jax.ShapeDtypeStruct((n_dp,) + tuple(dp_block), dp_send.dtype),
        ),
        in_specs=[pl.BlockSpec(memory_space=pl.ANY)] * 2,
        out_specs=(pl.BlockSpec(memory_space=pl.ANY), pl.BlockSpec(memory_space=pl.ANY)),
        scratch_shapes=[
            pltpu.SemaphoreType.DMA((n_ex + n_dp + n_dp,)),
            pltpu.SemaphoreType.DMA((n_ex + n_dp + n_dp,)),
            pltpu.SemaphoreType.DMA((2,)),
        ],
        compiler_params=pltpu.CompilerParams(collective_id=cid, has_side_effects=True),
    )(ex_send, dp_send)


def swiglu_forward(expert_rows, gate_up_full):
    projected = lax.dot_general(
        expert_rows,
        gate_up_full.reshape(expert_rows.shape[1], expert_rows.shape[2], -1),
        (((1, 2), (0, 1)), ((), ())),
        preferred_element_type=jnp.float32,
    )
    units = gate_up_full.shape[1] // 2
    gate_part = projected[:, :units]
    up_part = projected[:, units:]
    sigmoid_gate = jax.nn.sigmoid(gate_part)
    silu_gate = gate_part * sigmoid_gate
    hidden = (silu_gate * up_part).astype(jnp.bfloat16)
    return (hidden, gate_part, up_part, sigmoid_gate, silu_gate)


def weight_blocks(grad_rows, hidden):
    product = lax.dot_general(
        grad_rows, hidden, (((0,), (0,)), ((), ())), preferred_element_type=jnp.float32
    )
    parts = lax.axis_size("dp")
    blocks = (product * loss_scale).astype(jnp.bfloat16).reshape(-1, hidden.shape[1])
    return blocks.reshape(parts, blocks.shape[0] // parts, blocks.shape[1])


def shards(tokens, out_grad, routing, gate_probs, gate_up_weight, down_weight):
    peer_count = lax.axis_size("expert")
    local_count = gate_up_weight.shape[0]
    expert_count = peer_count * local_count
    tok_rows = tokens.shape[0]
    top_count = routing.shape[1]
    model_width = tokens.shape[1]
    capacity = max(2, 9 * tok_rows * top_count // (8 * expert_count))
    pair_count = tok_rows * top_count
    slot_count = expert_count * capacity
    flat_ids = routing.reshape(pair_count)
    onehot = (flat_ids[:, None] == jnp.arange(expert_count, dtype=jnp.int32)[None, :]).astype(
        jnp.int32
    )
    slot_rank = jnp.sum((jnp.cumsum(onehot, 0) - onehot) * onehot, 1)
    slot_of_pair = flat_ids * capacity + slot_rank
    pair_index = jnp.arange(pair_count, dtype=jnp.int32)
    matches = slot_of_pair[None, :] == jnp.arange(slot_count, dtype=jnp.int32)[:, None]
    filled = jnp.any(matches, axis=1)
    source = jnp.sum(jnp.where(matches, pair_index[None, :], 0), axis=1)
    token_of_slot = source // top_count
    probs_flat = gate_probs.reshape(pair_count)
    weight_slot = jnp.where(filled, probs_flat[source], jnp.float32(0.0))
    chunks = model_width // 128
    tok_chunks = tokens.reshape(tok_rows, chunks, 128)
    grad_chunks = out_grad.reshape(tok_rows, chunks, 128)
    send_rows = jnp.where(
        filled[:, None, None], tok_chunks[token_of_slot], jnp.zeros((), jnp.bfloat16)
    )
    send_grad = (
        weight_slot[:, None, None] * grad_chunks[token_of_slot].astype(jnp.float32)
    ).astype(jnp.bfloat16)
    block_shape = (peer_count, local_count * capacity * 2 * model_width // 128, 128)
    send_both = jnp.concatenate([send_rows, send_grad], axis=1).reshape(block_shape)
    gate_width = gate_up_weight.shape[2]
    joined = jnp.concatenate([gate_up_weight[0], down_weight[0]], axis=1)
    recv_both, gathered = exchange(send_both, joined, True, 0)
    recv_both = recv_both.reshape(slot_count, 2 * chunks, 128)
    expert_rows = recv_both[:, :chunks]
    grad_rows = recv_both[:, chunks:]
    full_joined = gathered.reshape(-1, joined.shape[1])
    full_gate_up = full_joined[:, :gate_width]
    full_down = full_joined[:, gate_width:]
    hidden, gate_part, up_part, sigmoid_gate, silu_gate = swiglu_forward(expert_rows, full_gate_up)
    produced = lax.dot_general(
        hidden, full_down, (((1,), (1,)), ((), ())), preferred_element_type=jnp.float32
    )
    down_parts = weight_blocks(grad_rows, hidden)
    hidden_grad = lax.dot_general(
        grad_rows,
        full_down.reshape(chunks, 128, -1),
        (((1, 2), (0, 1)), ((), ())),
        preferred_element_type=jnp.float32,
    )
    pre_grad = jnp.concatenate(
        [
            hidden_grad * up_part * sigmoid_gate * (1.0 + gate_part * (1.0 - sigmoid_gate)),
            hidden_grad * silu_gate,
        ],
        axis=1,
    ).astype(jnp.bfloat16)
    input_grad = lax.dot_general(
        pre_grad, full_gate_up, (((1,), (1,)), ((), ())), preferred_element_type=jnp.float32
    )
    back_both = jnp.concatenate(
        [
            produced.astype(jnp.bfloat16).reshape(slot_count, chunks, 128),
            input_grad.astype(jnp.bfloat16).reshape(slot_count, chunks, 128),
        ],
        axis=1,
    ).reshape(block_shape)
    returned, down_recv = exchange(back_both, down_parts, False, 1)
    pairs = returned.reshape(slot_count, 2 * chunks, 128)[slot_of_pair]
    out_pairs = pairs[:, :chunks]
    grad_pairs = pairs[:, chunks:]
    weighted = probs_flat[:, None, None] * out_pairs.astype(jnp.float32)
    mixed = jnp.sum(weighted.reshape(tok_rows, top_count, model_width), axis=1).astype(jnp.bfloat16)
    token_grad = jnp.sum(
        grad_pairs.astype(jnp.float32).reshape(tok_rows, top_count, model_width), axis=1
    ).astype(jnp.bfloat16)
    down_grad = jnp.sum(down_recv.astype(jnp.float32), axis=0)[None].astype(jnp.bfloat16)
    return (mixed, token_grad, down_grad)


def solution(mesh):
    in_specs = (
        P(("dp", "expert"), None),
        P(("dp", "expert"), None),
        P(("dp", "expert"), None),
        P(("dp", "expert"), None),
        P("expert", "dp", None),
        P("expert", "dp", None),
    )
    out_specs = (P(("dp", "expert"), None), P(("dp", "expert"), None), P("expert", "dp", None))
    return jax.shard_map(shards, mesh=mesh, in_specs=in_specs, out_specs=out_specs, check_vma=False)
```
